768 devices in a mesh: lat: 12 (over z_lo, core), lon: 16 (over z_hi, y), lev: 4 (over x).
Axes of the slice: x: 4, y: 8, z: 12 (z_hi: 2, z_lo: 6; z = z_hi * 6 + z_lo), core: 2. Of those that a mesh axis runs over, the one named last changes fastest.
Arguments:
- tokens: bfloat16 [4, 72, 384, 512], P('lev', 'lat', 'lon'), may hold values from -6 to 6
- norm_gain: float32 [2, 2, 512], replicated, may hold values from 0.25 to 1.75
- norm_offset: float32 [2, 2, 512], replicated, may hold values from -3 to 3
- w_qkv: bfloat16 [2, 512, 1536], replicated, may hold values from -0.25 to 0.25
- w_proj: bfloat16 [2, 512, 512], replicated, may hold values from -0.25 to 0.25
- w_up: bfloat16 [2, 512, 1024], replicated, may hold values from -0.25 to 0.25
- w_down: bfloat16 [2, 1024, 512], replicated, may hold values from -0.1875 to 0.1875
- rel_bias: float32 [2, 16, 37], replicated, may hold values from -4 to 720
Outputs:
- result: bfloat16 [4, 72, 384, 512], P('lev', 'lat', 'lon')
The draws below stay inside these ranges and needn't reach their ends.
All inputs are finite; a program needn't handle non-finite values.
Results may differ from the reference program's by a relative error of at most 0.015.
Values may be sent and summed in bfloat16 or wider, within the bound.
No kernel may reach another device: no remote copies, remote signals or barrier semaphores. Data moves between devices by JAX's collectives and lax.ppermute only.
A program may use at most 64 MiB of HBM per device.

```python
import jax
import jax.numpy as jnp
from jax import lax

D = 512
HID = 1024
HEADS = 16
HEAD_DIM = 32
WLAT = 6
WLON = 12
WLEV = 2
LAT = 72
LON = 384
LEV = 4


def draw_rel_bias(key, part):
    key_scale = jax.random.fold_in(key, 11)
    relative_count = 2 * WLAT + 2 * WLON + 2 * WLEV - 3
    return jnp.clip(0.7 * jax.random.normal(key_scale, (2, HEADS, relative_count), jnp.float32), -4.0, 4.0)


def steps_of(own_key, dims, pieces, smallest, largest):
    factor_of = 1.0
    for position, blocks in pieces:
        heights = jax.random.uniform(jax.random.fold_in(jax.random.fold_in(own_key, 6), position), (blocks,), jnp.float32, smallest / len(pieces), largest / len(pieces))
        factor_of = factor_of * jnp.repeat(jnp.exp(heights), dims[position] // blocks).reshape((-1,) + (1,) * (len(dims) - 1 - position))
    return factor_of


def normal_values(own_key, shape, scale, most, cuts=(), kind=jnp.bfloat16):
    array = scale * jax.random.normal(own_key, shape, jnp.float32)
    if cuts:
        array = array * steps_of(own_key, shape, cuts, -0.22, 0.18)
    return jnp.clip(array, -most, most).astype(kind)


def setup_inputs(seed: int = 0) -> dict:
    key_list = jax.random.split(jax.random.key(seed), 9)
    tokens = normal_values(key_list[0], (LEV, LAT, LON, D), 1.0, 6.0, ((0, 4), (1, 12), (2, 16)))
    norm_gain = jnp.clip(1.0 + 0.15 * jax.random.normal(key_list[1], (2, 2, D), jnp.float32), 0.25, 1.75)
    norm_offset = normal_values(key_list[2], (2, 2, D), 0.5, 3.0, (), jnp.float32)
    w_qkv = normal_values(key_list[3], (2, D, 3 * D), D ** -0.5, 0.25)
    w_proj = normal_values(key_list[4], (2, D, D), D ** -0.5, 0.25)
    w_up = normal_values(key_list[5], (2, D, HID), D ** -0.5, 0.25)
    w_down = normal_values(key_list[6], (2, HID, D), HID ** -0.5, 0.1875)
    rel_bias = draw_rel_bias(jax.random.fold_in(key_list[8], 71), 0)
    return {"tokens": tokens, "norm_gain": norm_gain, "norm_offset": norm_offset, "w_qkv": w_qkv, "w_proj": w_proj, "w_up": w_up, "w_down": w_down, "rel_bias": rel_bias}


EPS = 1e-05

def layer_norm(values, norm_scale, norm_shift):
    average = lax.optimization_barrier(jnp.mean(values, axis=-1, keepdims=True))
    centered = values - average
    variance = lax.optimization_barrier(jnp.mean(centered * centered, axis=-1, keepdims=True))
    return centered * lax.rsqrt(variance + EPS) * norm_scale + norm_shift

def relative_bias(bias_table):
    positions = jnp.arange(WLEV * WLAT * WLON)
    level_index = positions // (WLAT * WLON)
    lat_index = positions // WLON % WLAT
    lon_index = positions % WLON
    index_lat = lat_index[:, None] - lat_index[None, :] + WLAT - 1
    index_lon = lon_index[:, None] - lon_index[None, :] + 2 * WLAT - 1 + WLON - 1
    index_lev = level_index[:, None] - level_index[None, :] + 2 * WLAT + 2 * WLON - 2 + WLEV - 1
    columns = jnp.arange(bias_table.shape[-1])
    onehot = (index_lat[..., None] == columns).astype(jnp.float32) + (index_lon[..., None] == columns).astype(jnp.float32) + (index_lev[..., None] == columns).astype(jnp.float32)
    return jnp.einsum('ijr,hr->hij', onehot, bias_table.astype(jnp.float32), precision=lax.Precision.HIGHEST)

def block_group(group_tokens, region_rows, gains, offsets, weight_qkv, weight_proj, weight_up, weight_down, bias_full):
    lon_total = group_tokens.shape[2]
    lon_wins = lon_total // WLON
    window_size = WLEV * WLAT * WLON
    tokens_f = group_tokens.astype(jnp.float32).reshape(-1, D)
    normed = layer_norm(tokens_f, gains[0], offsets[0]).astype(jnp.bfloat16)
    packed = jnp.dot(normed, weight_qkv, preferred_element_type=jnp.float32).astype(jnp.bfloat16)
    packed = packed.reshape(WLEV, WLAT, lon_wins, WLON, 3, HEADS, HEAD_DIM)
    packed = packed.transpose(2, 4, 5, 0, 1, 3, 6).reshape(lon_wins, 3, HEADS, window_size, HEAD_DIM)
    packed = packed.astype(jnp.float32)
    scores = jnp.einsum('whqd,whkd->whqk', packed[:, 0], packed[:, 1]) * (1.0 / HEAD_DIM ** 0.5) + bias_full[None]
    row_region = region_rows[jnp.arange(window_size) // WLON % WLAT]
    same_region = row_region[:, None] == row_region[None, :]
    scores = jnp.where(same_region[None, None], scores, -1e+30)
    row_max = lax.optimization_barrier(jnp.max(scores, axis=-1, keepdims=True))
    exponent = jnp.exp(scores - row_max)
    attention = (exponent / lax.optimization_barrier(jnp.sum(exponent, axis=-1, keepdims=True))).astype(jnp.bfloat16)
    mixture = jnp.einsum('whqk,whkd->whqd', attention.astype(jnp.float32), packed[:, 2]).astype(jnp.bfloat16)
    mixture = mixture.reshape(lon_wins, HEADS, WLEV, WLAT, WLON, HEAD_DIM).transpose(2, 3, 0, 4, 1, 5).reshape(-1, D)
    residual = (tokens_f + jnp.dot(mixture, weight_proj, preferred_element_type=jnp.float32)).astype(jnp.bfloat16)
    normed_mlp = layer_norm(residual.astype(jnp.float32), gains[1], offsets[1]).astype(jnp.bfloat16)
    hidden = jax.nn.gelu(jnp.dot(normed_mlp, weight_up, preferred_element_type=jnp.float32)).astype(jnp.bfloat16)
    output = residual.astype(jnp.float32) + jnp.dot(hidden, weight_down, preferred_element_type=jnp.float32)
    return output.astype(jnp.bfloat16).reshape(WLEV, WLAT, lon_total, D)

def run_block(state_in, block_index, region, norm_gain, norm_offset, w_qkv, w_proj, w_up, w_down, rel_bias):
    groups = state_in.reshape(LEV // WLEV, WLEV, LAT // WLAT, WLAT, LON, D).transpose(0, 2, 1, 3, 4, 5)
    groups = groups.reshape(-1, WLEV, WLAT, LON, D)
    region_groups = jnp.tile(region.reshape(LAT // WLAT, WLAT), (LEV // WLEV, 1))
    bias_full = relative_bias(rel_bias[block_index])

    def apply_group(members):
        return block_group(members[0], members[1], norm_gain[block_index], norm_offset[block_index], w_qkv[block_index], w_proj[block_index], w_up[block_index], w_down[block_index], bias_full)
    outputs = lax.map(apply_group, (groups, region_groups))
    outputs = outputs.reshape(LEV // WLEV, LAT // WLAT, WLEV, WLAT, LON, D).transpose(0, 2, 1, 3, 4, 5)
    return outputs.reshape(LEV, LAT, LON, D)

def reference(tokens, norm_gain, norm_offset, w_qkv, w_proj, w_up, w_down, rel_bias):
    zero_region = jnp.zeros((LAT,), jnp.int32)
    first_pass = run_block(tokens, 0, zero_region, norm_gain, norm_offset, w_qkv, w_proj, w_up, w_down, rel_bias)
    half_lat = WLAT // 2
    half_lon = WLON // 2
    rolled = jnp.roll(first_pass, (-half_lat, -half_lon), axis=(1, 2))
    region = (jnp.arange(LAT) + half_lat >= LAT).astype(jnp.int32)
    second_pass = run_block(rolled, 1, region, norm_gain, norm_offset, w_qkv, w_proj, w_up, w_down, rel_bias)
    return jnp.roll(second_pass, (half_lat, half_lon), axis=(1, 2))
```

```python
import functools
import math

import jax
import jax.numpy as jnp
from jax import lax
from jax.experimental import pallas as pl
from jax.experimental.pallas import tpu as pltpu
from jax.sharding import PartitionSpec as P

D = 512
HID = 1024
HEADS = 16
HEAD_DIM = 32
WLAT = 6
WLON = 12
WLEV = 2
EPS = 1e-05

QROWS, QCOLS = WLAT // 2, WLON // 2
QTOK = WLEV * QROWS * QCOLS
QPAD = 48
WROWS = 4 * QPAD
KEYS = 256
PLANE = WLAT * WLON
GROUP = 128 // HEAD_DIM
GROUPS = HEADS // GROUP
FEAT = WLAT + WLON + WLEV
NEG = -1e30
ROOT = math.sqrt(HEAD_DIM)
AXES = ("lat", "lon", "lev")


def f32dot(a, b):
    return jnp.dot(a, b, preferred_element_type=jnp.float32)


def layer_norm(values, gain, offset):
    average = jnp.mean(values, axis=-1, keepdims=True)
    centered = values - average
    variance = jnp.mean(centered * centered, axis=-1, keepdims=True)
    return centered * lax.rsqrt(variance + EPS) * gain + offset


def attend(query, bias_q, keys, values, key_feat):
    n = query.shape[0]
    lane_head = lax.broadcasted_iota(jnp.int32, (n, 128), 1) // HEAD_DIM
    pad = jnp.zeros((KEYS - WROWS, 128), jnp.bfloat16)
    ones = jnp.ones((KEYS, 128), jnp.bfloat16)
    outs = []
    for g in range(GROUPS):
        lanes = slice(g * 128, (g + 1) * 128)
        qg = query[:, lanes]
        lhs = jnp.concatenate(
            [
                jnp.concatenate(
                    [
                        jnp.where(lane_head == h, qg, jnp.zeros_like(qg)),
                        bias_q[:, (g * GROUP + h) * 128 : (g * GROUP + h + 1) * 128],
                    ],
                    axis=1,
                )
                for h in range(GROUP)
            ],
            axis=0,
        )
        rhs = jnp.concatenate(
            [jnp.concatenate([keys[:, lanes], pad], axis=0), key_feat], axis=1
        )
        scores = lax.dot_general(
            lhs, rhs, (((1,), (1,)), ((), ())), preferred_element_type=jnp.float32
        )
        top = jnp.max(scores, axis=-1, keepdims=True)
        weight = jnp.exp2((scores - top) * (math.log2(math.e) / ROOT)).astype(jnp.bfloat16)
        vals = jnp.concatenate(
            [jnp.concatenate([values[:, lanes], pad], axis=0), ones], axis=1
        )
        both = f32dot(weight, vals)
        total = both[:n]
        for h in range(1, GROUP):
            here = jnp.concatenate([lane_head, lane_head], axis=1) == h
            total = jnp.where(here, both[h * n : (h + 1) * n], total)
        outs.append((total[:, :128] / total[:, 128:]).astype(jnp.bfloat16))
    return jnp.concatenate(outs, axis=1)


def finish(tokens, mixture, gain, offset, w_proj, w_up, w_down):
    residual = (tokens + f32dot(mixture, w_proj)).astype(jnp.bfloat16).astype(jnp.float32)
    normed = layer_norm(residual, gain, offset).astype(jnp.bfloat16)
    hidden = jax.nn.gelu(f32dot(normed, w_up)).astype(jnp.bfloat16)
    return (residual + f32dot(hidden, w_down)).astype(jnp.bfloat16)


def block_params(b, gain, offset, w_qkv, w_proj, w_up, w_down):
    return tuple(ref.at[b] for ref in (gain, offset, w_qkv, w_proj, w_up, w_down))


def first_kernel(
    own, other, pick, pos, table, key_feat, gain, offset, w_qkv, w_proj, w_up, w_down, out
):
    gain, offset, w_qkv, w_proj, w_up, w_down = block_params(
        0, gain, offset, w_qkv, w_proj, w_up, w_down
    )
    tokens = f32dot(pick[:, : 2 * PLANE], own[...]) + f32dot(pick[:, 2 * PLANE :], other[...])
    normed = layer_norm(tokens, gain[0:1], offset[0:1]).astype(jnp.bfloat16)
    packed = f32dot(normed, w_qkv[...]).astype(jnp.bfloat16)
    bias_q = f32dot(pos[...], table[...]).astype(jnp.bfloat16)
    mixture = attend(
        packed[:, :D], bias_q, packed[:, D : 2 * D], packed[:, 2 * D :], key_feat[...]
    )
    out[...] = finish(
        tokens, mixture, gain[1:2], offset[1:2], w_proj[...], w_up[...], w_down[...]
    )


def second_kernel(
    own, lon_a, lon_b, lat_a, lat_b, place, pos, table, key_feat,
    gain, offset, w_qkv, w_proj, w_up, w_down, keep, send, kv,
):
    gain, offset, w_qkv, w_proj, w_up, w_down = block_params(
        1, gain, offset, w_qkv, w_proj, w_up, w_down
    )
    tokens = own[...].astype(jnp.float32)
    g0, o0 = gain[0:1], offset[0:1]
    normed = layer_norm(tokens, g0, o0).astype(jnp.bfloat16)
    query = f32dot(normed, w_qkv[:, :D]).astype(jnp.bfloat16)
    kv[:WROWS] = f32dot(normed, w_qkv[:, D:]).astype(jnp.bfloat16)
    base = WROWS
    for ref in (lon_a, lon_b, lat_a, lat_b):
        more = layer_norm(ref[...].astype(jnp.float32), g0, o0).astype(jnp.bfloat16)
        kv[base : base + ref.shape[0]] = f32dot(more, w_qkv[:, D:]).astype(jnp.bfloat16)
        base += ref.shape[0]
    bias_q = f32dot(pos[...], table[...]).astype(jnp.bfloat16)
    parts = []
    for sb in range(2):
        for sa in range(2):
            quad = (2 * sb + sa) * QPAD
            lat0 = 2 * WROWS + sa * WROWS
            rows = (
                quad,
                WROWS + (2 * sb + sa) * QPAD,
                lat0 + sb * QPAD,
                lat0 + (2 + sb) * QPAD,
            )
            window = jnp.concatenate([kv[r : r + QPAD] for r in rows], axis=0)
            parts.append(
                attend(
                    query[quad : quad + QPAD],
                    bias_q[quad : quad + QPAD],
                    window[:, :D],
                    window[:, D:],
                    key_feat[2 * sb + sa],
                )
            )
    mixture = jnp.concatenate(parts, axis=0)
    result = finish(
        tokens, mixture, gain[1:2], offset[1:2], w_proj[...], w_up[...], w_down[...]
    )
    keep[...] = f32dot(place[:PLANE], result).astype(jnp.bfloat16)
    send[...] = f32dot(place[PLANE:], result).astype(jnp.bfloat16)


def merge_kernel(mine, theirs, spread, out):
    both = f32dot(spread[:, :PLANE], mine[...]) + f32dot(spread[:, PLANE:], theirs[...])
    out[...] = both.astype(jnp.bfloat16)


def call(kernel, outs, args, scratch=(), flops=0, vmem=24 << 20):
    return pl.pallas_call(
        kernel,
        out_shape=[jax.ShapeDtypeStruct(s, jnp.bfloat16) for s in outs],
        in_specs=[pl.BlockSpec(memory_space=pltpu.VMEM)] * len(args),
        out_specs=[pl.BlockSpec(memory_space=pltpu.VMEM)] * len(outs),
        scratch_shapes=list(scratch),
        compiler_params=pltpu.CompilerParams(vmem_limit_bytes=vmem),
        cost_estimate=pl.CostEstimate(flops=flops, bytes_accessed=1 << 20, transcendentals=0),
    )(*args)


def routes(mesh_shape):
    n_lat, n_lon, n_lev = mesh_shape

    def pairs(move):
        flat = lambda i, j, l: ((i % n_lat) * n_lon + j % n_lon) * n_lev + l
        return [
            (flat(i, j, l), flat(*move(i, j, l)))
            for i in range(n_lat)
            for j in range(n_lon)
            for l in range(n_lev)
        ]

    return {
        "lev": pairs(lambda i, j, l: (i, j, l ^ 1)),
        "lon": pairs(lambda i, j, l: (i, j + 1 if (l + j) % 2 else j - 1, l)),
        "lat_a": pairs(lambda i, j, l: (i ^ 1, j, l)),
        "lat_b": pairs(lambda i, j, l: (i + 1 if i % 2 else i - 1, j, l)),
    }


def onehot(rows, columns, count):
    hit = rows[:, None] == jnp.arange(columns)[None, :]
    return jnp.where(hit, count[:, None], 0).astype(jnp.bfloat16)


def position_features(a, o, lv, width):
    lane = jnp.arange(width)[None, :]
    hit = (lane == a[:, None]) | (lane == (WLAT + o)[:, None]) | (lane == (WLAT + WLON + lv)[:, None])
    return hit


def bias_table(rel_bias, wrap):
    scaled = rel_bias * ROOT
    hi = lax.reduce_precision(scaled, 8, 7)
    mid = lax.reduce_precision(scaled - hi, 8, 7)
    low = lax.reduce_precision(scaled - hi - mid, 8, 7)
    pieces = jnp.stack([hi, mid, low]).astype(jnp.bfloat16)
    r = jnp.arange(FEAT)[:, None]
    c = jnp.arange(FEAT)[None, :]
    lat = (r < WLAT) & (c < WLAT)
    lon = (r >= WLAT) & (c >= WLAT) & (r < WLAT + WLON) & (c < WLAT + WLON)
    lev = (r >= WLAT + WLON) & (c >= WLAT + WLON)
    start = jnp.where(lat, WLAT - 1, jnp.where(lon, 2 * WLAT - 1 + WLON - 1, 2 * WLAT + 2 * WLON - 2 + WLEV - 1))
    index = jnp.where(lat | lon | lev, start + r - c, -1)
    pick = (index[None] == jnp.arange(rel_bias.shape[-1])[:, None, None]).astype(jnp.bfloat16)
    spread = jnp.einsum("sht,trc->rhsc", pieces, pick, preferred_element_type=jnp.float32)
    spread = spread.reshape(FEAT, HEADS, 3 * FEAT)
    spread = jnp.pad(spread, ((0, 32 - FEAT), (0, 0), (0, 128 - 3 * FEAT)))
    row = jnp.arange(32)[:, None, None]
    lane = jnp.arange(128)[None, None, :]
    flag = jnp.where(lane == 3 * FEAT, NEG, jnp.where(lane == 3 * FEAT + 1, NEG * wrap, 0.0))
    spread = jnp.where(row == FEAT, flag, spread)
    return spread.astype(jnp.bfloat16).reshape(32, HEADS * 128)


def query_features(a, o, lv):
    lane = jnp.arange(32)[None, :]
    return (position_features(a, o, lv, 32) | (lane == FEAT)).astype(jnp.bfloat16)


def key_features(a, o, lv, real, far):
    lane = jnp.arange(128)
    folded = jnp.where(lane < 3 * FEAT, lane % FEAT, -1)[None, :]
    hit = (folded == a[:, None]) | (folded == (WLAT + o)[:, None]) | (folded == (WLAT + WLON + lv)[:, None])
    lane = lane[None, :]
    hit = (hit & real[:, None]) | ((lane == 3 * FEAT) & ~real[:, None])
    return (hit | ((lane == 3 * FEAT + 1) & far[:, None])).astype(jnp.bfloat16)


def shards(mesh_shape, tokens, norm_gain, norm_offset, w_qkv, w_proj, w_up, w_down, rel_bias):
    send_to = routes(mesh_shape)
    swap = lambda x, name: lax.ppermute(x, AXES, send_to[name])
    i, j, l = (lax.axis_index(name) for name in AXES)
    lv = l % 2
    side = (l + j) % 2
    odd = i % 2
    wrap = ((i == 0) | (i == mesh_shape[0] - 1)).astype(jnp.float32)

    plane = tokens[0]
    other = swap(lax.dynamic_slice_in_dim(plane, WLON * (1 - side), WLON, 1).reshape(PLANE, D), "lev")

    row = jnp.arange(WROWS)
    sb, sa = row // (2 * QPAD), row // QPAD % 2
    t = row % QPAD
    t_lv, t_a, t_o = t // (QROWS * QCOLS), t // QCOLS % QROWS, t % QCOLS
    real = (t < QTOK).astype(jnp.int32)
    bottom = jnp.where(sa == 0, 1 - odd, odd)
    right = jnp.where(sb == 0, 1 - side, side)
    a, o = QROWS * bottom + t_a, QCOLS * right + t_o
    lon_cols = 2 * WLON
    mine = t_lv == lv
    source = jnp.where(mine, a * lon_cols + WLON * side + o, 2 * PLANE + a * WLON + o)
    pick = onehot(source, 3 * PLANE, real)
    pos = query_features(a, o, jnp.minimum(t_lv, 1))
    fill = lambda x: jnp.pad(x, (0, KEYS - WROWS))
    no = jnp.zeros((KEYS,), bool)
    feat_first = key_features(fill(a), fill(o), fill(t_lv), fill(real) > 0, no)

    weights = (norm_gain, norm_offset, w_qkv, w_proj, w_up, w_down)
    (first,) = call(
        first_kernel,
        [(WROWS, D)],
        (plane.reshape(2 * PLANE, D), other, pick, pos, bias_table(rel_bias[0], 0.0), feat_first)
        + weights,
        flops=2 * 10**9,
    )

    lon_a = swap(first[: 2 * QPAD], "lev")
    lon_b = swap(first[2 * QPAD :], "lon")

    def strip(k):
        at = lambda x, q: x[q * QPAD : (q + 1) * QPAD]
        return jnp.concatenate([at(first, k), at(first, 2 + k), at(lon_a, k), at(lon_b, k)], axis=0)

    lat_a = swap(strip(0), "lat_a")
    lat_b = swap(strip(1), "lat_b")

    key = jnp.arange(KEYS)
    k_part, k_t = key // QPAD, key % QPAD
    k_lv, k_a, k_o = k_t // (QROWS * QCOLS), k_t // QCOLS % QROWS, k_t % QCOLS
    k_real = (k_t < QTOK) & (key < WROWS)
    feats = []
    for s_lon in range(2):
        for s_lat in range(2):
            own_low = (1 - odd) if s_lat == 1 else odd
            own_right = (1 - side) if s_lon == 1 else side
            low = jnp.where(k_part >= 2, 1 - own_low, own_low)
            east = jnp.where(k_part % 2 == 1, 1 - own_right, own_right)
            feats.append(
                key_features(
                    QROWS * low + k_a,
                    QCOLS * east + k_o,
                    k_lv,
                    k_real,
                    (k_part >= 2) & k_real & (s_lat == 1),
                )
            )
    pos2 = query_features(
        QROWS * (1 - bottom) + t_a, QCOLS * (1 - right) + t_o, jnp.minimum(t_lv, 1)
    )
    out_row = jnp.arange(2 * PLANE)
    level = jnp.where(out_row < PLANE, lv, 1 - lv)
    w_a, w_o = out_row % PLANE // WLON, out_row % WLON
    q_sa = jnp.where(w_a // QROWS == 1 - odd, 0, 1)
    q_sb = jnp.where(w_o // QCOLS == 1 - side, 0, 1)
    target = (
        (2 * q_sb + q_sa) * QPAD
        + level * QROWS * QCOLS
        + w_a % QROWS * QCOLS
        + w_o % QCOLS
    )
    place = onehot(target, WROWS, jnp.ones_like(target))
    keep, send = call(
        second_kernel,
        [(PLANE, D), (PLANE, D)],
        (first, lon_a, lon_b, lat_a, lat_b, place, pos2, bias_table(rel_bias[1], wrap), jnp.stack(feats))
        + weights,
        scratch=[pltpu.VMEM((4 * WROWS, 2 * D), jnp.bfloat16)],
        flops=3 * 10**9,
    )
    theirs = swap(send, "lev")
    f_a, f_c = out_row // lon_cols, out_row % lon_cols
    inside = f_c // WLON == side
    at = f_a * WLON + f_c % WLON
    spread = onehot(jnp.where(inside, at, PLANE + at), 2 * PLANE, jnp.ones_like(at))
    (result,) = call(merge_kernel, [(2 * PLANE, D)], (keep, theirs, spread), flops=10**8)
    return result.reshape(1, WLAT, lon_cols, D)


def solution(mesh):
    shape = tuple(mesh.shape[name] for name in AXES)
    return jax.shard_map(
        functools.partial(shards, shape),
        mesh=mesh,
        in_specs=(P("lev", "lat", "lon", None), P(), P(), P(), P(), P(), P(), P()),
        out_specs=P("lev", "lat", "lon", None),
        check_vma=False,
    )
```

```python
import functools
import math

import jax
import jax.numpy as jnp
from jax import lax
from jax.experimental import pallas as pl
from jax.experimental.pallas import tpu as pltpu
from jax.sharding import PartitionSpec as P


D = 512
HEADS = 16
HEAD_DIM = 32
WLAT = 6
WLON = 12
WLEV = 2
EPS = 1e-05

QROWS, QCOLS = WLAT // 2, WLON // 2
QPAD = 48
HALF = 2 * QPAD
WROWS = 4 * QPAD
KEYS = 256
PLANE = WLAT * WLON
GROUP = 128 // HEAD_DIM
GROUPS = HEADS // GROUP
FEAT = WLAT + WLON + WLEV
FROWS = 24
NEG = -1e30
ROOT = math.sqrt(HEAD_DIM)
AXES = ("lat", "lon", "lev")


def f32dot(a, b):
    return jnp.dot(a, b, preferred_element_type=jnp.float32)


def layer_norm(values, gain, offset):
    average = jnp.mean(values, axis=-1, keepdims=True)
    centered = values - average
    variance = jnp.mean(centered * centered, axis=-1, keepdims=True)
    return centered * lax.rsqrt(variance + EPS) * gain + offset


def attend(query, bias_q, keys, values, key_feat):
    n = query.shape[0]
    lane_head = lax.broadcasted_iota(jnp.int32, (n, 128), 1) // HEAD_DIM
    pad = jnp.zeros((KEYS - WROWS, 128), jnp.bfloat16)
    ones = jnp.ones((KEYS, 128), jnp.bfloat16)
    outs = []
    for g in range(GROUPS):
        lanes = slice(g * 128, (g + 1) * 128)
        qg = query[:, lanes]
        lhs = jnp.concatenate(
            [
                jnp.concatenate(
                    [
                        jnp.where(lane_head == h, qg, jnp.zeros_like(qg)),
                        bias_q[:, (g * GROUP + h) * 128 : (g * GROUP + h + 1) * 128],
                    ],
                    axis=1,
                )
                for h in range(GROUP)
            ],
            axis=0,
        )
        rhs = jnp.concatenate(
            [jnp.concatenate([keys[:, lanes], pad], axis=0), key_feat], axis=1
        )
        scores = lax.dot_general(
            lhs, rhs, (((1,), (1,)), ((), ())), preferred_element_type=jnp.float32
        )
        top = jnp.max(scores, axis=-1, keepdims=True)
        weight = jnp.exp2((scores - top) * (math.log2(math.e) / ROOT)).astype(jnp.bfloat16)
        vals = jnp.concatenate(
            [jnp.concatenate([values[:, lanes], pad], axis=0), ones], axis=1
        )
        both = f32dot(weight, vals)
        total = both[:n]
        for h in range(1, GROUP):
            here = jnp.concatenate([lane_head, lane_head], axis=1) == h
            total = jnp.where(here, both[h * n : (h + 1) * n], total)
        outs.append((total[:, :128] / total[:, 128:]).astype(jnp.bfloat16))
    return jnp.concatenate(outs, axis=1)


def finish(tokens, mixture, gain, offset, w_proj, w_up, w_down):
    residual = (tokens + f32dot(mixture, w_proj)).astype(jnp.bfloat16).astype(jnp.float32)
    normed = layer_norm(residual, gain, offset).astype(jnp.bfloat16)
    hidden = jax.nn.gelu(f32dot(normed, w_up)).astype(jnp.bfloat16)
    return (residual + f32dot(hidden, w_down)).astype(jnp.bfloat16)


def place_of_device():
    i, j, l = (lax.axis_index(name) for name in AXES)
    wrap = (i == 0) | (i == lax.axis_size("lat") - 1)
    return l % 2, (l + j) % 2, i % 2, wrap


def steps(values, size, count):
    total = jnp.zeros_like(values)
    for k in range(1, count):
        total = total + (values >= k * size).astype(jnp.int32)
    return total


def column(rows):
    return lax.broadcasted_iota(jnp.int32, (rows, 1), 0)


def split_token(t):
    lv = steps(t, QROWS * QCOLS, 3)
    rest = t - lv * (QROWS * QCOLS)
    a = steps(rest, QCOLS, QROWS)
    return lv, a, rest - a * QCOLS


def split_window(w):
    a = steps(w, WLON, WLAT)
    return a, w - a * WLON


def onehot(index, columns):
    lane = lax.broadcasted_iota(jnp.int32, (index.shape[0], columns), 1)
    return (lane == index).astype(jnp.float32).astype(jnp.bfloat16)


def features(a, o, lv, real, width, copies, flags=()):
    lane = lax.broadcasted_iota(jnp.int32, (a.shape[0], width), 1)
    hit = jnp.zeros(lane.shape, jnp.float32)
    for k in range(copies):
        base = k * FEAT
        here = (lane == base + a) | (lane == base + WLAT + o) | (lane == base + WLAT + WLON + lv)
        hit = jnp.where(here, 1.0, hit)
    hit = jnp.where(real, hit, 0.0)
    for k, flag in enumerate(flags):
        hit = jnp.where((lane == copies * FEAT + k) & flag, 1.0, hit)
    return hit.astype(jnp.bfloat16)


def window_rows(side, odd, shifted):
    row = column(WROWS)
    quad = steps(row, QPAD, 4)
    sb = (quad >= 2).astype(jnp.int32)
    sa = quad - 2 * sb
    lv, a, o = split_token(row - quad * QPAD)
    low = jnp.where(sa == 0, 1 - odd, odd)
    east = jnp.where(sb == 0, 1 - side, side)
    if shifted:
        return lv, QROWS * (1 - low) + a, QCOLS * (1 - east) + o
    return lv, QROWS * low + a, QCOLS * east + o


def query_bias(b, spots, table, wrap, bias):
    lane = lax.broadcasted_iota(jnp.int32, (1, 256), 1) % 128
    masks = jnp.where(lane == 3 * FEAT, NEG, 0.0)
    if wrap is not None:
        masks = jnp.where((lane == 3 * FEAT + 1) & wrap, NEG, masks)
    for h in range(0, HEADS, 2):
        pair = [table[pl.ds(b * HEADS + h + k, FROWS, stride=2 * HEADS), :] for k in range(2)]
        rows = jnp.concatenate(pair, axis=1).astype(jnp.bfloat16)
        bias[:, h * 128 : (h + 2) * 128] = (f32dot(spots, rows) + masks).astype(jnp.bfloat16)


def cut_kernel(plane, out):
    _, side, _, _ = place_of_device()
    a, o = split_window(column(PLANE))
    source = a * (2 * WLON) + WLON * (1 - side) + o
    out[...] = f32dot(onehot(source, 2 * PLANE), plane[...]).astype(jnp.bfloat16)


def start_weights(b, sources, targets, sems):
    copies = [
        pltpu.make_async_copy(src.at[b], dst, sems.at[k])
        for k, (src, dst) in enumerate(zip(sources, targets, strict=True))
    ]
    for copy in copies:
        copy.start()
    return copies


def fill_table(rel_bias, table):
    scaled = rel_bias[...] * ROOT
    hi = scaled.astype(jnp.bfloat16)
    rest = scaled - hi.astype(jnp.float32)
    mid = rest.astype(jnp.bfloat16)
    low = (rest - mid.astype(jnp.float32)).astype(jnp.bfloat16)
    rows, count = rel_bias.shape
    n = lax.broadcasted_iota(jnp.int32, (1, FROWS * 128), 1)
    r, lane = n // 128, n % 128
    piece = steps(lane, FEAT, 4)
    c = lane - piece * FEAT
    lat = (r < WLAT) & (c < WLAT)
    lon = (r >= WLAT) & (c >= WLAT) & (r < WLAT + WLON) & (c < WLAT + WLON)
    lev = (r >= WLAT + WLON) & (r < FEAT) & (c >= WLAT + WLON)
    start = jnp.where(
        lat,
        WLAT - 1,
        jnp.where(lon, 2 * WLAT + WLON - 2, 2 * WLAT + 2 * WLON + WLEV - 3),
    )
    index = jnp.where(lat | lon | lev, start + r - c, -1)
    entry = lax.broadcasted_iota(jnp.int32, (count, FROWS * 128), 0)
    total = jnp.zeros((rows, FROWS * 128), jnp.float32)
    for k, part in enumerate((hi, mid, low)):
        hit = entry == jnp.where(piece == k, index, -1)
        total = total + f32dot(part, jnp.where(hit, 1.0, 0.0).astype(jnp.bfloat16))
    for r in range(FROWS):
        table[r * rows : (r + 1) * rows] = total[:, r * 128 : (r + 1) * 128]


def prepare_first(
    rel_bias, w_qkv, w_proj, w_up, w_down,
    pick, key_feat, bias, table, v_qkv, v_proj, v_up, v_down, sems,
):
    copies = start_weights(
        0, (w_qkv, w_proj, w_up, w_down), (v_qkv, v_proj, v_up, v_down), sems
    )
    fill_table(rel_bias, table)
    level, side, odd, _ = place_of_device()
    lv, a, o = window_rows(side, odd, False)
    mine = a * (2 * WLON) + WLON * side + o
    source = jnp.where(lv == level, mine, 2 * PLANE + a * WLON + o)
    source = jnp.where(lv < WLEV, source, -1)
    pick[...] = onehot(source, 3 * PLANE)
    real = lv < WLEV
    spots = features(a, o, lv, real, FROWS, 1)
    query_bias(0, spots, table, None, bias)
    key_feat[:WROWS] = features(a, o, lv, real, 128, 3, [~real])
    lane = lax.broadcasted_iota(jnp.int32, (KEYS - WROWS, 128), 1)
    key_feat[WROWS:] = jnp.where(lane == 3 * FEAT, 1.0, 0.0).astype(jnp.bfloat16)
    for copy in copies:
        copy.wait()


def prepare_second(
    after, table, w_qkv, w_proj, w_up, w_down,
    key_feat, bias, place, spread, v_qkv, v_proj, v_up, v_down, sems,
):
    del after
    copies = start_weights(
        1, (w_qkv, w_proj, w_up, w_down), (v_qkv, v_proj, v_up, v_down), sems
    )
    level, side, odd, wrap = place_of_device()
    lv, a, o = window_rows(side, odd, True)
    spots = features(a, o, lv, lv < WLEV, FROWS, 1)
    query_bias(1, spots, table, wrap, bias)
    row = column(KEYS)
    part = steps(row, QPAD, 5)
    lv, a, o = split_token(row - part * QPAD)
    real = (lv < WLEV) & (part < 4)
    across_lat = (part >= 2).astype(jnp.int32)
    across_lon = ((part == 1) | (part == 3)).astype(jnp.int32)
    for s_lon in range(2):
        for s_lat in range(2):
            own_low = odd if s_lat == 0 else 1 - odd
            own_east = side if s_lon == 0 else 1 - side
            low = jnp.where(across_lat == 1, 1 - own_low, own_low)
            east = jnp.where(across_lon == 1, 1 - own_east, own_east)
            flags = [~real] + ([real & (across_lat == 1)] if s_lat else [])
            key_feat[2 * s_lon + s_lat] = features(
                QROWS * low + a, QCOLS * east + o, lv, real, 128, 3, flags
            )
    row = column(2 * PLANE)
    other = (row >= PLANE).astype(jnp.int32)
    a, o = split_window(row - other * PLANE)
    at_level = jnp.where(other == 1, 1 - level, level)
    low, east = (a >= QROWS).astype(jnp.int32), (o >= QCOLS).astype(jnp.int32)
    sa = jnp.where(low == 1 - odd, 0, 1)
    sb = jnp.where(east == 1 - side, 0, 1)
    target = (2 * sb + sa) * QPAD + at_level * (QROWS * QCOLS)
    place[...] = onehot(target + (a - QROWS * low) * QCOLS + o - QCOLS * east, WROWS)
    a = steps(row, 2 * WLON, WLAT)
    c = row - a * (2 * WLON)
    right = (c >= WLON).astype(jnp.int32)
    at = a * WLON + c - WLON * right
    spread[...] = onehot(jnp.where(right == side, at, PLANE + at), 2 * PLANE)
    for copy in copies:
        copy.wait()


def first_kernel(
    own, other, pick, bias, key_feat, gain, offset, w_qkv, w_proj, w_up, w_down, out, near, far
):
    gain, offset = gain.at[0], offset.at[0]
    tokens = f32dot(pick[:, : 2 * PLANE], own[...]) + f32dot(pick[:, 2 * PLANE :], other[...])
    normed = layer_norm(tokens, gain[0:1], offset[0:1]).astype(jnp.bfloat16)
    packed = f32dot(normed, w_qkv[...]).astype(jnp.bfloat16)
    mixture = attend(
        packed[:, :D], bias, packed[:, D : 2 * D], packed[:, 2 * D :], key_feat[...]
    )
    result = finish(
        tokens, mixture, gain[1:2], offset[1:2], w_proj[...], w_up[...], w_down[...]
    )
    out[...] = result
    near[...] = result[:HALF]
    far[...] = result[HALF:]


def strip_kernel(own, lon, lat_a, lat_b):
    for k, out in enumerate((lat_a, lat_b)):
        for at, (ref, quad) in enumerate(((own, k), (own, 2 + k), (lon, k))):
            out[at * QPAD : (at + 1) * QPAD] = ref[quad * QPAD : (quad + 1) * QPAD]


def corner_kernel(own, lon, lat_a, lat_b):
    _, _, _, wrap = place_of_device()
    lat_a[...] = lon[:QPAD]

    @pl.when(wrap)
    def _():
        lat_b[...] = own[3 * QPAD :]

    @pl.when(jnp.logical_not(wrap))
    def _():
        lat_b[...] = lon[QPAD:]


def near_kernel(
    own, lon, lat_a, lat_b, bias, key_feat,
    gain, offset, w_qkv, w_proj, w_up, w_down, done, query_far, kv_far, kv,
):
    gain, offset = gain.at[1], offset.at[1]
    g0, o0 = gain[0:1], offset[0:1]
    tokens = own[...].astype(jnp.float32)
    normed = layer_norm(tokens, g0, o0).astype(jnp.bfloat16)
    query = f32dot(normed, w_qkv[:, :D]).astype(jnp.bfloat16)
    kv[:WROWS] = f32dot(normed, w_qkv[:, D:]).astype(jnp.bfloat16)
    base = WROWS
    for ref in (lon, lat_a, lat_b):
        more = layer_norm(ref[...].astype(jnp.float32), g0, o0).astype(jnp.bfloat16)
        kv[base : base + ref.shape[0]] = f32dot(more, w_qkv[:, D:]).astype(jnp.bfloat16)
        base += ref.shape[0]
    parts = []
    for sa in range(2):
        lat = WROWS + HALF + sa * 3 * QPAD
        rows = (sa * QPAD, WROWS + sa * QPAD, lat, lat + 2 * QPAD)
        window = jnp.concatenate([kv[r : r + QPAD] for r in rows], axis=0)
        q = slice(sa * QPAD, (sa + 1) * QPAD)
        parts.append(attend(query[q], bias.at[q], window[:, :D], window[:, D:], key_feat[sa]))
        kv_far[2 * sa * QPAD : (2 * sa + 1) * QPAD] = kv[HALF + sa * QPAD : HALF + (sa + 1) * QPAD]
        kv_far[(2 * sa + 1) * QPAD : (2 * sa + 2) * QPAD] = kv[lat + QPAD : lat + 2 * QPAD]
    query_far[...] = query[HALF:]
    done[...] = finish(
        tokens[:HALF], jnp.concatenate(parts, axis=0), gain[1:2], offset[1:2],
        w_proj[...], w_up[...], w_down[...],
    )


def far_kernel(
    own, done, query, kv_near, lon, lat_a, lat_b, bias, key_feat, place,
    gain, offset, w_qkv, w_proj, w_up, w_down, keep, send,
):
    gain, offset = gain.at[1], offset.at[1]
    late = jnp.concatenate([lon[...], lat_a[...], lat_b[...]], axis=0).astype(jnp.float32)
    normed = layer_norm(late, gain[0:1], offset[0:1]).astype(jnp.bfloat16)
    kv = f32dot(normed, w_qkv[:, D:]).astype(jnp.bfloat16)
    parts = []
    for sa in range(2):
        near = 2 * sa * QPAD
        window = jnp.concatenate(
            [
                kv_near[near : near + QPAD],
                kv[sa * QPAD : (sa + 1) * QPAD],
                kv_near[near + QPAD : near + 2 * QPAD],
                kv[(2 + sa) * QPAD : (3 + sa) * QPAD],
            ],
            axis=0,
        )
        q = slice(sa * QPAD, (sa + 1) * QPAD)
        b = slice(HALF + sa * QPAD, HALF + (sa + 1) * QPAD)
        parts.append(attend(query[q], bias.at[b], window[:, :D], window[:, D:], key_feat[2 + sa]))
    result = finish(
        own[HALF:].astype(jnp.float32), jnp.concatenate(parts, axis=0), gain[1:2], offset[1:2],
        w_proj[...], w_up[...], w_down[...],
    )
    both = f32dot(place[:, :HALF], done[...]) + f32dot(place[:, HALF:], result)
    keep[...] = both[:PLANE].astype(jnp.bfloat16)
    send[...] = both[PLANE:].astype(jnp.bfloat16)


def merge_kernel(mine, theirs, spread, out):
    both = f32dot(spread[:, :PLANE], mine[...]) + f32dot(spread[:, PLANE:], theirs[...])
    out[...] = both.astype(jnp.bfloat16)


def call(kernel, outs, args, scratch=(), flops=0, skip=(), wide=(), vmem=24 << 20):
    specs = [
        pl.BlockSpec(memory_space=pltpu.HBM if k in skip else pltpu.VMEM) for k in range(len(args))
    ]
    return pl.pallas_call(
        kernel,
        out_shape=[
            jax.ShapeDtypeStruct(s, jnp.float32 if k in wide else jnp.bfloat16)
            for k, s in enumerate(outs)
        ],
        in_specs=specs,
        out_specs=[pl.BlockSpec(memory_space=pltpu.VMEM)] * len(outs),
        scratch_shapes=list(scratch),
        compiler_params=pltpu.CompilerParams(vmem_limit_bytes=vmem),
        cost_estimate=pl.CostEstimate(flops=flops, bytes_accessed=1 << 20, transcendentals=0),
    )(*args)


def routes(mesh_shape):
    n_lat, n_lon, n_lev = mesh_shape

    def pairs(move):
        flat = lambda i, j, l: ((i % n_lat) * n_lon + j % n_lon) * n_lev + l
        return [
            (flat(i, j, l), flat(*move(i, j, l)))
            for i in range(n_lat)
            for j in range(n_lon)
            for l in range(n_lev)
        ]

    lat_b = lambda i: i + 1 if i % 2 else i - 1
    lon_b = lambda j, l: j + 1 if (l + j) % 2 else j - 1
    ends = (0, n_lat - 1)
    return {
        "lev": pairs(lambda i, j, l: (i, j, l ^ 1)),
        "lon": pairs(lambda i, j, l: (i, lon_b(j, l), l)),
        "lat_a": pairs(lambda i, j, l: (i ^ 1, j, l)),
        "lat_b": pairs(lambda i, j, l: (lat_b(i), j, l)),
        "corner": pairs(lambda i, j, l: (lat_b(i), lon_b(j, l) if i in ends else j, l)),
    }


def shards(mesh_shape, tokens, norm_gain, norm_offset, w_qkv, w_proj, w_up, w_down, rel_bias):
    send_to = routes(mesh_shape)
    swap = lambda x, name: lax.ppermute(x, AXES, send_to[name])
    norms = (norm_gain, norm_offset)
    raw = tuple(
        pltpu.with_memory_space_constraint(w, pltpu.HBM) for w in (w_qkv, w_proj, w_up, w_down)
    )
    shapes = [w.shape[1:] for w in raw]
    sems = [pltpu.SemaphoreType.DMA((len(raw),))]

    plane = tokens.reshape(2 * PLANE, D)
    (cut,) = call(cut_kernel, [(PLANE, D)], (plane,), flops=10**7)
    other = swap(cut, "lev")
    pick, feat_first, bias_first, table, *weights = call(
        prepare_first,
        [(WROWS, 3 * PLANE), (KEYS, 128), (WROWS, HEADS * 128), (FROWS * 2 * HEADS, 128)] + shapes,
        (rel_bias.reshape(2 * HEADS, rel_bias.shape[-1]),) + raw,
        scratch=sems,
        flops=10**8,
        skip=(1, 2, 3, 4),
        wide=(3,),
    )
    first, near, far = call(
        first_kernel,
        [(WROWS, D), (HALF, D), (HALF, D)],
        (plane, other, pick, bias_first, feat_first) + norms + tuple(weights),
        flops=2 * 10**9,
    )

    lon_b = swap(far, "lon")
    lon_a = swap(near, "lev")
    feat_second, bias_second, place, spread, *weights = call(
        prepare_second,
        [(4, KEYS, 128), (WROWS, HEADS * 128), (2 * PLANE, WROWS), (2 * PLANE, 2 * PLANE)] + shapes,
        (first, table) + raw,
        scratch=sems,
        flops=10**8,
        skip=(2, 3, 4, 5),
    )
    weights = norms + tuple(weights)
    strip_a, strip_b = call(strip_kernel, [(3 * QPAD, D)] * 2, (first, lon_a), flops=10**6)
    lat_b = swap(strip_b, "lat_b")
    lat_a = swap(strip_a, "lat_a")
    done, query_far, kv_far = call(
        near_kernel,
        [(HALF, D), (HALF, D), (WROWS, 2 * D)],
        (first, lon_a, lat_a, lat_b, bias_second, feat_second) + weights,
        scratch=[pltpu.VMEM((WROWS + HALF + 6 * QPAD, 2 * D), jnp.bfloat16)],
        flops=2 * 10**9,
    )

    corner_a, corner_b = call(corner_kernel, [(QPAD, D)] * 2, (first, lon_b), flops=10**6)
    corner_b = swap(corner_b, "corner")
    corner_a = swap(corner_a, "lat_a")
    keep, send = call(
        far_kernel,
        [(PLANE, D), (PLANE, D)],
        (first, done, query_far, kv_far, lon_b, corner_a, corner_b, bias_second, feat_second, place)
        + weights,
        flops=2 * 10**9,
    )
    theirs = swap(send, "lev")
    (result,) = call(merge_kernel, [(2 * PLANE, D)], (keep, theirs, spread), flops=10**8)
    return result.reshape(1, WLAT, 2 * WLON, D)


def solution(mesh):
    shape = tuple(mesh.shape[name] for name in AXES)
    return jax.shard_map(
        functools.partial(shards, shape),
        mesh=mesh,
        in_specs=(P("lev", "lat", "lon", None), P(), P(), P(), P(), P(), P(), P()),
        out_specs=P("lev", "lat", "lon", None),
        check_vma=False,
    )
```

```python
import functools
import math

import jax
import jax.numpy as jnp
from jax import lax
from jax.experimental import pallas as pl
from jax.experimental.pallas import tpu as pltpu
from jax.sharding import PartitionSpec as P


D = 512
HEADS = 16
HEAD_DIM = 32
WLAT = 6
WLON = 12
WLEV = 2
EPS = 1e-05

QROWS, QCOLS = WLAT // 2, WLON // 2
QPAD = 48
HALF = 2 * QPAD
WROWS = 4 * QPAD
KEYS = 256
PLANE = WLAT * WLON
GROUP = 128 // HEAD_DIM
GROUPS = HEADS // GROUP
FEAT = WLAT + WLON + WLEV
FROWS = 24
NEG = -1e30
ROOT = math.sqrt(HEAD_DIM)
AXES = ("lat", "lon", "lev")


def f32dot(a, b):
    return jnp.dot(a, b, preferred_element_type=jnp.float32)


def layer_norm(values, gain, offset):
    average = jnp.mean(values, axis=-1, keepdims=True)
    centered = values - average
    variance = jnp.mean(centered * centered, axis=-1, keepdims=True)
    return centered * lax.rsqrt(variance + EPS) * gain + offset


def attend(query, bias_q, keys, values, key_feat):
    n = query.shape[0]
    lane_head = lax.broadcasted_iota(jnp.int32, (n, 128), 1) // HEAD_DIM
    pad = jnp.zeros((KEYS - WROWS, 128), jnp.bfloat16)
    ones = jnp.ones((KEYS, 128), jnp.bfloat16)
    outs = []
    for g in range(GROUPS):
        lanes = slice(g * 128, (g + 1) * 128)
        qg = query[:, lanes]
        lhs = jnp.concatenate(
            [
                jnp.concatenate(
                    [
                        jnp.where(lane_head == h, qg, jnp.zeros_like(qg)),
                        bias_q[:, (g * GROUP + h) * 128 : (g * GROUP + h + 1) * 128],
                    ],
                    axis=1,
                )
                for h in range(GROUP)
            ],
            axis=0,
        )
        rhs = jnp.concatenate(
            [jnp.concatenate([keys[:, lanes], pad], axis=0), key_feat], axis=1
        )
        scores = lax.dot_general(
            lhs, rhs, (((1,), (1,)), ((), ())), preferred_element_type=jnp.float32
        )
        top = jnp.max(scores, axis=-1, keepdims=True)
        weight = jnp.exp2((scores - top) * (math.log2(math.e) / ROOT)).astype(jnp.bfloat16)
        vals = jnp.concatenate(
            [jnp.concatenate([values[:, lanes], pad], axis=0), ones], axis=1
        )
        both = f32dot(weight, vals)
        total = both[:n]
        for h in range(1, GROUP):
            here = jnp.concatenate([lane_head, lane_head], axis=1) == h
            total = jnp.where(here, both[h * n : (h + 1) * n], total)
        outs.append((total[:, :128] / total[:, 128:]).astype(jnp.bfloat16))
    return jnp.concatenate(outs, axis=1)


def finish(tokens, mixture, gain, offset, w_proj, w_up, w_down):
    residual = (tokens + f32dot(mixture, w_proj)).astype(jnp.bfloat16).astype(jnp.float32)
    normed = layer_norm(residual, gain, offset).astype(jnp.bfloat16)
    hidden = jax.nn.gelu(f32dot(normed, w_up)).astype(jnp.bfloat16)
    return (residual + f32dot(hidden, w_down)).astype(jnp.bfloat16)


def place_of_device():
    i, j, l = (lax.axis_index(name) for name in AXES)
    wrap = (i == 0) | (i == lax.axis_size("lat") - 1)
    return l % 2, (l + j) % 2, i % 2, wrap


def steps(values, size, count):
    total = jnp.zeros_like(values)
    for k in range(1, count):
        total = total + (values >= k * size).astype(jnp.int32)
    return total


def column(rows):
    return lax.broadcasted_iota(jnp.int32, (rows, 1), 0)


def split_token(t):
    lv = steps(t, QROWS * QCOLS, 3)
    rest = t - lv * (QROWS * QCOLS)
    a = steps(rest, QCOLS, QROWS)
    return lv, a, rest - a * QCOLS


def split_window(w):
    a = steps(w, WLON, WLAT)
    return a, w - a * WLON


def onehot(index, columns):
    lane = lax.broadcasted_iota(jnp.int32, (index.shape[0], columns), 1)
    return (lane == index).astype(jnp.float32).astype(jnp.bfloat16)


def features(a, o, lv, real, width, copies, flags=()):
    lane = lax.broadcasted_iota(jnp.int32, (a.shape[0], width), 1)
    hit = jnp.zeros(lane.shape, jnp.float32)
    for k in range(copies):
        base = k * FEAT
        here = (lane == base + a) | (lane == base + WLAT + o) | (lane == base + WLAT + WLON + lv)
        hit = jnp.where(here, 1.0, hit)
    hit = jnp.where(real, hit, 0.0)
    for k, flag in enumerate(flags):
        hit = jnp.where((lane == copies * FEAT + k) & flag, 1.0, hit)
    return hit.astype(jnp.bfloat16)


def window_rows(side, odd, shifted):
    row = column(WROWS)
    quad = steps(row, QPAD, 4)
    sb = (quad >= 2).astype(jnp.int32)
    sa = quad - 2 * sb
    lv, a, o = split_token(row - quad * QPAD)
    low = jnp.where(sa == 0, 1 - odd, odd)
    east = jnp.where(sb == 0, 1 - side, side)
    if shifted:
        return lv, QROWS * (1 - low) + a, QCOLS * (1 - east) + o
    return lv, QROWS * low + a, QCOLS * east + o


def query_bias(b, spots, table, wrap, bias):
    lane = lax.broadcasted_iota(jnp.int32, (1, 256), 1) % 128
    masks = jnp.where(lane == 3 * FEAT, NEG, 0.0)
    if wrap is not None:
        masks = jnp.where((lane == 3 * FEAT + 1) & wrap, NEG, masks)
    for h in range(0, HEADS, 2):
        pair = [table[pl.ds(b * HEADS + h + k, FROWS, stride=2 * HEADS), :] for k in range(2)]
        rows = jnp.concatenate(pair, axis=1).astype(jnp.bfloat16)
        bias[:, h * 128 : (h + 2) * 128] = (f32dot(spots, rows) + masks).astype(jnp.bfloat16)


def cut_kernel(plane, out):
    _, side, _, _ = place_of_device()
    a, o = split_window(column(PLANE))
    source = a * (2 * WLON) + WLON * (1 - side) + o
    out[...] = f32dot(onehot(source, 2 * PLANE), plane[...]).astype(jnp.bfloat16)


def start_weights(b, sources, targets, sems):
    copies = [
        pltpu.make_async_copy(src.at[b], dst, sems.at[k])
        for k, (src, dst) in enumerate(zip(sources, targets, strict=True))
    ]
    for copy in copies:
        copy.start()
    return copies


def fill_table(scaled, table):
    hi = scaled.astype(jnp.bfloat16)
    rest = scaled - hi.astype(jnp.float32)
    mid = rest.astype(jnp.bfloat16)
    low = (rest - mid.astype(jnp.float32)).astype(jnp.bfloat16)
    rows, count = scaled.shape
    width = FROWS * 128
    n = lax.broadcasted_iota(jnp.int32, (1, width), 1)
    r, c = n // 128, n % 128
    lat = (r < WLAT) & (c < WLAT)
    lon = (r >= WLAT) & (c >= WLAT) & (r < WLAT + WLON) & (c < WLAT + WLON)
    lev = (r >= WLAT + WLON) & (r < FEAT) & (c >= WLAT + WLON) & (c < FEAT)
    start = jnp.where(
        lat,
        WLAT - 1,
        jnp.where(lon, 2 * WLAT + WLON - 2, 2 * WLAT + 2 * WLON + WLEV - 3),
    )
    index = jnp.where(lat | lon | lev, start + r - c, -1)
    entry = lax.broadcasted_iota(jnp.int32, (count, width), 0)
    hit = jnp.where(entry == index, 1.0, 0.0).astype(jnp.bfloat16)
    found = f32dot(jnp.concatenate([hi, mid, low], axis=0), hit)
    total = found[:rows]
    for k in (1, 2):
        total = total + pltpu.roll(found[k * rows : (k + 1) * rows], k * FEAT, 1)
    for r in range(FROWS):
        table[r * rows : (r + 1) * rows] = total[:, r * 128 : (r + 1) * 128]


def prepare_first(
    rel_bias, w_qkv, w_proj, w_up, w_down,
    pick, key_feat, bias, table, v_qkv, v_proj, v_up, v_down, entries, sems,
):
    fetch = pltpu.make_async_copy(rel_bias, entries, sems.at[4])
    fetch.start()
    copies = start_weights(
        0, (w_qkv, w_proj, w_up, w_down), (v_qkv, v_proj, v_up, v_down), sems
    )
    level, side, odd, _ = place_of_device()
    lv, a, o = window_rows(side, odd, False)
    mine = a * (2 * WLON) + WLON * side + o
    source = jnp.where(lv == level, mine, 2 * PLANE + a * WLON + o)
    source = jnp.where(lv < WLEV, source, -1)
    pick[...] = onehot(source, 3 * PLANE)
    real = lv < WLEV
    spots = features(a, o, lv, real, FROWS, 1)
    key_feat[:WROWS] = features(a, o, lv, real, 128, 3, [~real])
    lane = lax.broadcasted_iota(jnp.int32, (KEYS - WROWS, 128), 1)
    key_feat[WROWS:] = jnp.where(lane == 3 * FEAT, 1.0, 0.0).astype(jnp.bfloat16)
    fetch.wait()
    fill_table(entries[...] * ROOT, table)
    query_bias(0, spots, table, None, bias)
    for copy in copies:
        copy.wait()


def prepare_second(
    own, table, gain, offset, w_qkv, w_proj, w_up, w_down,
    key_feat, bias, place, spread, query, kv, v_qkv, v_proj, v_up, v_down, sems,
):
    copies = start_weights(
        1, (w_qkv, w_proj, w_up, w_down), (v_qkv, v_proj, v_up, v_down), sems
    )
    level, side, odd, wrap = place_of_device()
    lv, a, o = window_rows(side, odd, True)
    spots = features(a, o, lv, lv < WLEV, FROWS, 1)
    query_bias(1, spots, table, wrap, bias)
    row = column(KEYS)
    part = steps(row, QPAD, 5)
    lv, a, o = split_token(row - part * QPAD)
    real = (lv < WLEV) & (part < 4)
    across_lat = (part >= 2).astype(jnp.int32)
    across_lon = ((part == 1) | (part == 3)).astype(jnp.int32)
    for s_lon in range(2):
        for s_lat in range(2):
            own_low = odd if s_lat == 0 else 1 - odd
            own_east = side if s_lon == 0 else 1 - side
            low = jnp.where(across_lat == 1, 1 - own_low, own_low)
            east = jnp.where(across_lon == 1, 1 - own_east, own_east)
            flags = [~real] + ([real & (across_lat == 1)] if s_lat else [])
            key_feat[2 * s_lon + s_lat] = features(
                QROWS * low + a, QCOLS * east + o, lv, real, 128, 3, flags
            )
    row = column(2 * PLANE)
    other = (row >= PLANE).astype(jnp.int32)
    a, o = split_window(row - other * PLANE)
    at_level = jnp.where(other == 1, 1 - level, level)
    low, east = (a >= QROWS).astype(jnp.int32), (o >= QCOLS).astype(jnp.int32)
    sa = jnp.where(low == 1 - odd, 0, 1)
    sb = jnp.where(east == 1 - side, 0, 1)
    target = (2 * sb + sa) * QPAD + at_level * (QROWS * QCOLS)
    place[...] = onehot(target + (a - QROWS * low) * QCOLS + o - QCOLS * east, WROWS)
    a = steps(row, 2 * WLON, WLAT)
    c = row - a * (2 * WLON)
    right = (c >= WLON).astype(jnp.int32)
    at = a * WLON + c - WLON * right
    spread[...] = onehot(jnp.where(right == side, at, PLANE + at), 2 * PLANE)
    normed = layer_norm(own[...].astype(jnp.float32), gain[1, 0:1], offset[1, 0:1])
    for copy in copies:
        copy.wait()
    packed = f32dot(normed.astype(jnp.bfloat16), v_qkv[...]).astype(jnp.bfloat16)
    query[...] = packed[:, :D]
    kv[...] = packed[:, D:]


def first_kernel(
    own, other, pick, bias, key_feat, gain, offset, w_qkv, w_proj, w_up, w_down, out, near, far
):
    gain, offset = gain.at[0], offset.at[0]
    tokens = f32dot(pick[:, : 2 * PLANE], own[...]) + f32dot(pick[:, 2 * PLANE :], other[...])
    normed = layer_norm(tokens, gain[0:1], offset[0:1]).astype(jnp.bfloat16)
    packed = f32dot(normed, w_qkv[...]).astype(jnp.bfloat16)
    mixture = attend(
        packed[:, :D], bias, packed[:, D : 2 * D], packed[:, 2 * D :], key_feat[...]
    )
    result = finish(
        tokens, mixture, gain[1:2], offset[1:2], w_proj[...], w_up[...], w_down[...]
    )
    out[...] = result
    near[...] = result[:HALF]
    far[...] = result[HALF:]


def strip_kernel(own, lon, lat_a, lat_b):
    for k, out in enumerate((lat_a, lat_b)):
        for at, (ref, quad) in enumerate(((own, k), (own, 2 + k), (lon, k))):
            out[at * QPAD : (at + 1) * QPAD] = ref[quad * QPAD : (quad + 1) * QPAD]


def corner_kernel(own, lon, lat_a, lat_b):
    _, _, _, wrap = place_of_device()
    lat_a[...] = lon[:QPAD]

    @pl.when(wrap)
    def _():
        lat_b[...] = own[3 * QPAD :]

    @pl.when(jnp.logical_not(wrap))
    def _():
        lat_b[...] = lon[QPAD:]


def near_kernel(
    own, query, kv_own, lon, lat_a, lat_b, bias, key_feat,
    gain, offset, w_qkv, w_proj, w_up, w_down, done, kv_far, kv,
):
    gain, offset = gain.at[1], offset.at[1]
    base = 0
    for ref in (lon, lat_a, lat_b):
        more = layer_norm(ref[...].astype(jnp.float32), gain[0:1], offset[0:1])
        kv[base : base + ref.shape[0]] = f32dot(more.astype(jnp.bfloat16), w_qkv[:, D:]).astype(
            jnp.bfloat16
        )
        base += ref.shape[0]
    parts = []
    for sa in range(2):
        q = slice(sa * QPAD, (sa + 1) * QPAD)
        lat = HALF + sa * 3 * QPAD
        window = jnp.concatenate(
            [kv_own[q], kv[q], kv[lat : lat + QPAD], kv[lat + 2 * QPAD : lat + 3 * QPAD]], axis=0
        )
        parts.append(attend(query[q], bias.at[q], window[:, :D], window[:, D:], key_feat[sa]))
        kv_far[sa * QPAD : (sa + 1) * QPAD] = kv[lat + QPAD : lat + 2 * QPAD]
    done[...] = finish(
        own[:HALF].astype(jnp.float32), jnp.concatenate(parts, axis=0), gain[1:2], offset[1:2],
        w_proj[...], w_up[...], w_down[...],
    )


def far_kernel(
    own, done, query, kv_own, kv_lat, lon, lat_a, lat_b, bias, key_feat, place,
    gain, offset, w_qkv, w_proj, w_up, w_down, keep, send,
):
    gain, offset = gain.at[1], offset.at[1]
    late = jnp.concatenate([lon[...], lat_a[...], lat_b[...]], axis=0).astype(jnp.float32)
    normed = layer_norm(late, gain[0:1], offset[0:1]).astype(jnp.bfloat16)
    kv = f32dot(normed, w_qkv[:, D:]).astype(jnp.bfloat16)
    parts = []
    for sa in range(2):
        q = slice(sa * QPAD, (sa + 1) * QPAD)
        b = slice(HALF + sa * QPAD, HALF + (sa + 1) * QPAD)
        window = jnp.concatenate(
            [kv_own[b], kv[q], kv_lat[q], kv[(2 + sa) * QPAD : (3 + sa) * QPAD]], axis=0
        )
        parts.append(attend(query[b], bias.at[b], window[:, :D], window[:, D:], key_feat[2 + sa]))
    result = finish(
        own[HALF:].astype(jnp.float32), jnp.concatenate(parts, axis=0), gain[1:2], offset[1:2],
        w_proj[...], w_up[...], w_down[...],
    )
    both = f32dot(place[:, :HALF], done[...]) + f32dot(place[:, HALF:], result)
    keep[...] = both[:PLANE].astype(jnp.bfloat16)
    send[...] = both[PLANE:].astype(jnp.bfloat16)


def merge_kernel(mine, theirs, spread, out):
    both = f32dot(spread[:, :PLANE], mine[...]) + f32dot(spread[:, PLANE:], theirs[...])
    out[...] = both.astype(jnp.bfloat16)


def call(kernel, outs, args, scratch=(), flops=0, skip=(), wide=(), vmem=24 << 20):
    specs = [
        pl.BlockSpec(memory_space=pltpu.HBM if k in skip else pltpu.VMEM) for k in range(len(args))
    ]
    return pl.pallas_call(
        kernel,
        out_shape=[
            jax.ShapeDtypeStruct(s, jnp.float32 if k in wide else jnp.bfloat16)
            for k, s in enumerate(outs)
        ],
        in_specs=specs,
        out_specs=[pl.BlockSpec(memory_space=pltpu.VMEM)] * len(outs),
        scratch_shapes=list(scratch),
        compiler_params=pltpu.CompilerParams(vmem_limit_bytes=vmem),
        cost_estimate=pl.CostEstimate(flops=flops, bytes_accessed=1 << 20, transcendentals=0),
    )(*args)


def routes(mesh_shape):
    n_lat, n_lon, n_lev = mesh_shape

    def pairs(move):
        flat = lambda i, j, l: ((i % n_lat) * n_lon + j % n_lon) * n_lev + l
        return [
            (flat(i, j, l), flat(*move(i, j, l)))
            for i in range(n_lat)
            for j in range(n_lon)
            for l in range(n_lev)
        ]

    lat_b = lambda i: i + 1 if i % 2 else i - 1
    lon_b = lambda j, l: j + 1 if (l + j) % 2 else j - 1
    ends = (0, n_lat - 1)
    return {
        "lev": pairs(lambda i, j, l: (i, j, l ^ 1)),
        "lon": pairs(lambda i, j, l: (i, lon_b(j, l), l)),
        "lat_a": pairs(lambda i, j, l: (i ^ 1, j, l)),
        "lat_b": pairs(lambda i, j, l: (lat_b(i), j, l)),
        "corner": pairs(lambda i, j, l: (lat_b(i), lon_b(j, l) if i in ends else j, l)),
    }


def shards(mesh_shape, tokens, norm_gain, norm_offset, w_qkv, w_proj, w_up, w_down, rel_bias):
    send_to = routes(mesh_shape)
    swap = lambda x, name: lax.ppermute(x, AXES, send_to[name])
    norms = (norm_gain, norm_offset)
    raw = tuple(
        pltpu.with_memory_space_constraint(w, pltpu.HBM) for w in (w_qkv, w_proj, w_up, w_down)
    )
    shapes = [w.shape[1:] for w in raw]
    sems = [pltpu.SemaphoreType.DMA((len(raw) + 1,))]

    plane = tokens.reshape(2 * PLANE, D)
    (cut,) = call(cut_kernel, [(PLANE, D)], (plane,), flops=10**7)
    other = swap(cut, "lev")
    entries = rel_bias.reshape(2 * HEADS, rel_bias.shape[-1])
    pick, feat_first, bias_first, table, *weights = call(
        prepare_first,
        [(WROWS, 3 * PLANE), (KEYS, 128), (WROWS, HEADS * 128), (FROWS * 2 * HEADS, 128)] + shapes,
        (pltpu.with_memory_space_constraint(entries, pltpu.HBM),) + raw,
        scratch=[pltpu.VMEM(entries.shape, jnp.float32)] + sems,
        flops=10**8,
        skip=(0, 1, 2, 3, 4),
        wide=(3,),
    )
    first, near, far = call(
        first_kernel,
        [(WROWS, D), (HALF, D), (HALF, D)],
        (plane, other, pick, bias_first, feat_first) + norms + tuple(weights),
        flops=2 * 10**9,
    )

    lon_a = swap(near, "lev")
    lon_b = swap(far, "lon")
    feat_second, bias_second, place, spread, query, kv_own, *weights = call(
        prepare_second,
        [(4, KEYS, 128), (WROWS, HEADS * 128), (2 * PLANE, WROWS), (2 * PLANE, 2 * PLANE)]
        + [(WROWS, D), (WROWS, 2 * D)]
        + shapes,
        (first, table) + norms + raw,
        scratch=sems,
        flops=10**9,
        skip=(4, 5, 6, 7),
    )
    weights = norms + tuple(weights)
    strip_a, strip_b = call(strip_kernel, [(3 * QPAD, D)] * 2, (first, lon_a), flops=10**6)
    lat_b = swap(strip_b, "lat_b")
    lat_a = swap(strip_a, "lat_a")
    done, kv_lat = call(
        near_kernel,
        [(HALF, D), (HALF, 2 * D)],
        (first, query, kv_own, lon_a, lat_a, lat_b, bias_second, feat_second) + weights,
        scratch=[pltpu.VMEM((HALF + 6 * QPAD, 2 * D), jnp.bfloat16)],
        flops=2 * 10**9,
    )

    corner_a, corner_b = call(corner_kernel, [(QPAD, D)] * 2, (first, lon_b), flops=10**6)
    corner_b = swap(corner_b, "corner")
    corner_a = swap(corner_a, "lat_a")
    keep, send = call(
        far_kernel,
        [(PLANE, D), (PLANE, D)],
        (first, done, query, kv_own, kv_lat, lon_b, corner_a, corner_b)
        + (bias_second, feat_second, place)
        + weights,
        flops=2 * 10**9,
    )
    theirs = swap(send, "lev")
    (result,) = call(merge_kernel, [(2 * PLANE, D)], (keep, theirs, spread), flops=10**8)
    return result.reshape(1, WLAT, 2 * WLON, D)


def solution(mesh):
    shape = tuple(mesh.shape[name] for name in AXES)
    return jax.shard_map(
        functools.partial(shards, shape),
        mesh=mesh,
        in_specs=(P("lev", "lat", "lon", None), P(), P(), P(), P(), P(), P(), P()),
        out_specs=P("lev", "lat", "lon", None),
        check_vma=False,
    )
```

```python
import functools
import math

import jax
import jax.numpy as jnp
from jax import lax
from jax.experimental import pallas as pl
from jax.experimental.pallas import tpu as pltpu
from jax.sharding import PartitionSpec as P


D = 512
HEADS = 16
HEAD_DIM = 32
WLAT = 6
WLON = 12
WLEV = 2
EPS = 1e-05

QROWS, QCOLS = WLAT // 2, WLON // 2
QPAD = 48
HALF = 2 * QPAD
WROWS = 4 * QPAD
KEYS = 256
PLANE = WLAT * WLON
GROUP = 128 // HEAD_DIM
GROUPS = HEADS // GROUP
FEAT = WLAT + WLON + WLEV
FROWS = 24
NEG = -1e30
ROOT = math.sqrt(HEAD_DIM)
AXES = ("lat", "lon", "lev")


def f32dot(a, b):
    return jnp.dot(a, b, preferred_element_type=jnp.float32)


def layer_norm(values, gain, offset):
    average = jnp.mean(values, axis=-1, keepdims=True)
    centered = values - average
    variance = jnp.mean(centered * centered, axis=-1, keepdims=True)
    return centered * lax.rsqrt(variance + EPS) * gain + offset


def attend(query, bias_q, keys, values, key_feat):
    n = query.shape[0]
    lane_head = lax.broadcasted_iota(jnp.int32, (n, 128), 1) // HEAD_DIM
    pad = jnp.zeros((KEYS - WROWS, 128), jnp.bfloat16)
    ones = jnp.ones((KEYS, 128), jnp.bfloat16)
    outs = []
    for g in range(GROUPS):
        lanes = slice(g * 128, (g + 1) * 128)
        qg = query[:, lanes]
        lhs = jnp.concatenate(
            [
                jnp.concatenate(
                    [
                        jnp.where(lane_head == h, qg, jnp.zeros_like(qg)),
                        bias_q[:, (g * GROUP + h) * 128 : (g * GROUP + h + 1) * 128],
                    ],
                    axis=1,
                )
                for h in range(GROUP)
            ],
            axis=0,
        )
        rhs = jnp.concatenate(
            [jnp.concatenate([keys[:, lanes], pad], axis=0), key_feat], axis=1
        )
        scores = lax.dot_general(
            lhs, rhs, (((1,), (1,)), ((), ())), preferred_element_type=jnp.float32
        )
        top = jnp.max(scores, axis=-1, keepdims=True)
        weight = jnp.exp2((scores - top) * (math.log2(math.e) / ROOT)).astype(jnp.bfloat16)
        vals = jnp.concatenate(
            [jnp.concatenate([values[:, lanes], pad], axis=0), ones], axis=1
        )
        both = f32dot(weight, vals)
        total = both[:n]
        for h in range(1, GROUP):
            here = jnp.concatenate([lane_head, lane_head], axis=1) == h
            total = jnp.where(here, both[h * n : (h + 1) * n], total)
        outs.append((total[:, :128] / total[:, 128:]).astype(jnp.bfloat16))
    return jnp.concatenate(outs, axis=1)


def finish(tokens, mixture, gain, offset, w_proj, w_up, w_down):
    residual = (tokens + f32dot(mixture, w_proj)).astype(jnp.bfloat16).astype(jnp.float32)
    normed = layer_norm(residual, gain, offset).astype(jnp.bfloat16)
    hidden = jax.nn.gelu(f32dot(normed, w_up)).astype(jnp.bfloat16)
    return (residual + f32dot(hidden, w_down)).astype(jnp.bfloat16)


def place_of_device():
    i, j, l = (lax.axis_index(name) for name in AXES)
    wrap = (i == 0) | (i == lax.axis_size("lat") - 1)
    return l % 2, (l + j) % 2, i % 2, wrap


def steps(values, size, count):
    total = jnp.zeros_like(values)
    for k in range(1, count):
        total = total + (values >= k * size).astype(jnp.int32)
    return total


def column(rows):
    return lax.broadcasted_iota(jnp.int32, (rows, 1), 0)


def split_token(t):
    lv = steps(t, QROWS * QCOLS, 3)
    rest = t - lv * (QROWS * QCOLS)
    a = steps(rest, QCOLS, QROWS)
    return lv, a, rest - a * QCOLS


def split_window(w):
    a = steps(w, WLON, WLAT)
    return a, w - a * WLON


def onehot(index, columns):
    lane = lax.broadcasted_iota(jnp.int32, (index.shape[0], columns), 1)
    return (lane == index).astype(jnp.float32).astype(jnp.bfloat16)


def features(a, o, lv, real, width, copies, flags=()):
    lane = lax.broadcasted_iota(jnp.int32, (a.shape[0], width), 1)
    hit = jnp.zeros(lane.shape, jnp.float32)
    for k in range(copies):
        base = k * FEAT
        here = (lane == base + a) | (lane == base + WLAT + o) | (lane == base + WLAT + WLON + lv)
        hit = jnp.where(here, 1.0, hit)
    hit = jnp.where(real, hit, 0.0)
    for k, flag in enumerate(flags):
        hit = jnp.where((lane == copies * FEAT + k) & flag, 1.0, hit)
    return hit.astype(jnp.bfloat16)


def window_rows(side, odd, shifted):
    row = column(WROWS)
    quad = steps(row, QPAD, 4)
    sb = (quad >= 2).astype(jnp.int32)
    sa = quad - 2 * sb
    lv, a, o = split_token(row - quad * QPAD)
    low = jnp.where(sa == 0, 1 - odd, odd)
    east = jnp.where(sb == 0, 1 - side, side)
    if shifted:
        return lv, QROWS * (1 - low) + a, QCOLS * (1 - east) + o
    return lv, QROWS * low + a, QCOLS * east + o


def query_bias(b, spots, table, wrap, bias):
    lane = lax.broadcasted_iota(jnp.int32, (1, 256), 1) % 128
    masks = jnp.where(lane == 3 * FEAT, NEG, 0.0)
    if wrap is not None:
        masks = jnp.where((lane == 3 * FEAT + 1) & wrap, NEG, masks)
    for h in range(0, HEADS, 2):
        pair = [table[pl.ds(b * HEADS + h + k, FROWS, stride=2 * HEADS), :] for k in range(2)]
        rows = jnp.concatenate(pair, axis=1).astype(jnp.bfloat16)
        bias[:, h * 128 : (h + 2) * 128] = (f32dot(spots, rows) + masks).astype(jnp.bfloat16)


def cut_kernel(plane, out):
    _, side, _, _ = place_of_device()
    a, o = split_window(column(PLANE))
    source = a * (2 * WLON) + WLON * (1 - side) + o
    out[...] = f32dot(onehot(source, 2 * PLANE), plane[...]).astype(jnp.bfloat16)


def start_weights(b, sources, targets, sems):
    copies = [
        pltpu.make_async_copy(src.at[b], dst, sems.at[k])
        for k, (src, dst) in enumerate(zip(sources, targets, strict=True))
    ]
    for copy in copies:
        copy.start()
    return copies


def fill_table(scaled, table):
    hi = scaled.astype(jnp.bfloat16)
    rest = scaled - hi.astype(jnp.float32)
    mid = rest.astype(jnp.bfloat16)
    low = (rest - mid.astype(jnp.float32)).astype(jnp.bfloat16)
    rows, count = scaled.shape
    width = FROWS * 128
    n = lax.broadcasted_iota(jnp.int32, (1, width), 1)
    r, c = n // 128, n % 128
    lat = (r < WLAT) & (c < WLAT)
    lon = (r >= WLAT) & (c >= WLAT) & (r < WLAT + WLON) & (c < WLAT + WLON)
    lev = (r >= WLAT + WLON) & (r < FEAT) & (c >= WLAT + WLON) & (c < FEAT)
    start = jnp.where(
        lat,
        WLAT - 1,
        jnp.where(lon, 2 * WLAT + WLON - 2, 2 * WLAT + 2 * WLON + WLEV - 3),
    )
    index = jnp.where(lat | lon | lev, start + r - c, -1)
    entry = lax.broadcasted_iota(jnp.int32, (count, width), 0)
    hit = jnp.where(entry == index, 1.0, 0.0).astype(jnp.bfloat16)
    found = f32dot(jnp.concatenate([hi, mid, low], axis=0), hit)
    total = found[:rows]
    for k in (1, 2):
        total = total + pltpu.roll(found[k * rows : (k + 1) * rows], k * FEAT, 1)
    for r in range(FROWS):
        table[r * rows : (r + 1) * rows] = total[:, r * 128 : (r + 1) * 128]


def prepare_first(
    rel_bias, w_qkv, w_proj, w_up, w_down,
    pick, key_feat, bias, table, v_qkv, v_proj, v_up, v_down, entries, sems,
):
    fetch = pltpu.make_async_copy(rel_bias, entries, sems.at[4])
    fetch.start()
    copies = start_weights(
        0, (w_qkv, w_proj, w_up, w_down), (v_qkv, v_proj, v_up, v_down), sems
    )
    level, side, odd, _ = place_of_device()
    lv, a, o = window_rows(side, odd, False)
    mine = a * (2 * WLON) + WLON * side + o
    source = jnp.where(lv == level, mine, 2 * PLANE + a * WLON + o)
    source = jnp.where(lv < WLEV, source, -1)
    pick[...] = onehot(source, 3 * PLANE)
    real = lv < WLEV
    spots = features(a, o, lv, real, FROWS, 1)
    key_feat[:WROWS] = features(a, o, lv, real, 128, 3, [~real])
    lane = lax.broadcasted_iota(jnp.int32, (KEYS - WROWS, 128), 1)
    key_feat[WROWS:] = jnp.where(lane == 3 * FEAT, 1.0, 0.0).astype(jnp.bfloat16)
    fetch.wait()
    fill_table(entries[...] * ROOT, table)
    query_bias(0, spots, table, None, bias)
    for copy in copies:
        copy.wait()


def on_half(early):
    i, j, l = (lax.axis_index(name) for name in AXES)
    here = (j < lax.axis_size("lon") // 2) & (i + j + l > 0)
    return here if early else jnp.logical_not(here)


def prepare_if(early, *refs):
    @pl.when(on_half(early))
    def _():
        prepare_second(*refs)


def with_prepared(kernel, common, count, *refs):
    sets = refs[common : common + count], refs[common + count : common + 2 * count]
    for early, prepared in zip((True, False), sets, strict=True):

        @pl.when(on_half(early))
        def _(prepared=prepared):
            kernel(*refs[:common], *prepared, *refs[common + 2 * count :])


def prepare_second(
    own, table, gain, offset, w_qkv, w_proj, w_up, w_down,
    key_feat, bias, place, spread, query, kv, v_qkv, v_proj, v_up, v_down, sems,
):
    copies = start_weights(
        1, (w_qkv, w_proj, w_up, w_down), (v_qkv, v_proj, v_up, v_down), sems
    )
    level, side, odd, wrap = place_of_device()
    lv, a, o = window_rows(side, odd, True)
    spots = features(a, o, lv, lv < WLEV, FROWS, 1)
    query_bias(1, spots, table, wrap, bias)
    row = column(KEYS)
    part = steps(row, QPAD, 5)
    lv, a, o = split_token(row - part * QPAD)
    real = (lv < WLEV) & (part < 4)
    across_lat = (part >= 2).astype(jnp.int32)
    across_lon = ((part == 1) | (part == 3)).astype(jnp.int32)
    for s_lon in range(2):
        for s_lat in range(2):
            own_low = odd if s_lat == 0 else 1 - odd
            own_east = side if s_lon == 0 else 1 - side
            low = jnp.where(across_lat == 1, 1 - own_low, own_low)
            east = jnp.where(across_lon == 1, 1 - own_east, own_east)
            flags = [~real] + ([real & (across_lat == 1)] if s_lat else [])
            key_feat[2 * s_lon + s_lat] = features(
                QROWS * low + a, QCOLS * east + o, lv, real, 128, 3, flags
            )
    row = column(2 * PLANE)
    other = (row >= PLANE).astype(jnp.int32)
    a, o = split_window(row - other * PLANE)
    at_level = jnp.where(other == 1, 1 - level, level)
    low, east = (a >= QROWS).astype(jnp.int32), (o >= QCOLS).astype(jnp.int32)
    sa = jnp.where(low == 1 - odd, 0, 1)
    sb = jnp.where(east == 1 - side, 0, 1)
    target = (2 * sb + sa) * QPAD + at_level * (QROWS * QCOLS)
    place[...] = onehot(target + (a - QROWS * low) * QCOLS + o - QCOLS * east, WROWS)
    a = steps(row, 2 * WLON, WLAT)
    c = row - a * (2 * WLON)
    right = (c >= WLON).astype(jnp.int32)
    at = a * WLON + c - WLON * right
    spread[...] = onehot(jnp.where(right == side, at, PLANE + at), 2 * PLANE)
    normed = layer_norm(own[...].astype(jnp.float32), gain[1, 0:1], offset[1, 0:1])
    for copy in copies:
        copy.wait()
    packed = f32dot(normed.astype(jnp.bfloat16), v_qkv[...]).astype(jnp.bfloat16)
    query[...] = packed[:, :D]
    kv[...] = packed[:, D:]


def first_kernel(
    own, other, pick, bias, key_feat, gain, offset, w_qkv, w_proj, w_up, w_down, out, near, far, last
):
    gain, offset = gain.at[0], offset.at[0]
    tokens = f32dot(pick[:, : 2 * PLANE], own[...]) + f32dot(pick[:, 2 * PLANE :], other[...])
    normed = layer_norm(tokens, gain[0:1], offset[0:1]).astype(jnp.bfloat16)
    packed = f32dot(normed, w_qkv[...]).astype(jnp.bfloat16)
    mixture = attend(
        packed[:, :D], bias, packed[:, D : 2 * D], packed[:, 2 * D :], key_feat[...]
    )
    result = finish(
        tokens, mixture, gain[1:2], offset[1:2], w_proj[...], w_up[...], w_down[...]
    )
    out[...] = result
    near[...] = result[:HALF]
    far[...] = result[HALF:]
    last[...] = result[3 * QPAD :]


def strip_kernel(own, lon, lat_a, lat_b):
    for k, out in enumerate((lat_a, lat_b)):
        for at, (ref, quad) in enumerate(((own, k), (own, 2 + k), (lon, k))):
            out[at * QPAD : (at + 1) * QPAD] = ref[quad * QPAD : (quad + 1) * QPAD]


def corner_kernel(lon, lat_a, lat_b):
    lat_a[...] = lon[:QPAD]
    lat_b[...] = lon[QPAD:]


def near_kernel(
    lon, lat_a, lat_b, gain, offset, query, kv_own, bias, key_feat, w_qkv, mixed, kv_far, kv,
):
    gain, offset = gain.at[1], offset.at[1]
    base = 0
    for ref in (lon, lat_a, lat_b):
        more = layer_norm(ref[...].astype(jnp.float32), gain[0:1], offset[0:1])
        kv[base : base + ref.shape[0]] = f32dot(more.astype(jnp.bfloat16), w_qkv[:, D:]).astype(
            jnp.bfloat16
        )
        base += ref.shape[0]
    parts = []
    for sa in range(2):
        q = slice(sa * QPAD, (sa + 1) * QPAD)
        lat = HALF + sa * 3 * QPAD
        window = jnp.concatenate(
            [kv_own[q], kv[q], kv[lat : lat + QPAD], kv[lat + 2 * QPAD : lat + 3 * QPAD]], axis=0
        )
        parts.append(attend(query[q], bias.at[q], window[:, :D], window[:, D:], key_feat[sa]))
        kv_far[sa * QPAD : (sa + 1) * QPAD] = kv[lat + QPAD : lat + 2 * QPAD]
    mixed[...] = jnp.concatenate(parts, axis=0)


def far_kernel(
    own, mixed, kv_lat, lon, lat_a, lat_b, lat_end, gain, offset,
    query, kv_own, bias, key_feat, place, w_qkv, w_proj, w_up, w_down, keep, send,
):
    gain, offset = gain.at[1], offset.at[1]
    _, _, _, wrap = place_of_device()
    corner = jnp.where(wrap, lat_end[...], lat_b[...])
    late = jnp.concatenate([lon[...], lat_a[...], corner], axis=0).astype(jnp.float32)
    normed = layer_norm(late, gain[0:1], offset[0:1]).astype(jnp.bfloat16)
    kv = f32dot(normed, w_qkv[:, D:]).astype(jnp.bfloat16)
    parts = []
    for sa in range(2):
        q = slice(sa * QPAD, (sa + 1) * QPAD)
        b = slice(HALF + sa * QPAD, HALF + (sa + 1) * QPAD)
        window = jnp.concatenate(
            [kv_own[b], kv[q], kv_lat[q], kv[(2 + sa) * QPAD : (3 + sa) * QPAD]], axis=0
        )
        parts.append(attend(query[b], bias.at[b], window[:, :D], window[:, D:], key_feat[2 + sa]))
    result = finish(
        own[...].astype(jnp.float32), jnp.concatenate([mixed[...]] + parts, axis=0), gain[1:2],
        offset[1:2], w_proj[...], w_up[...], w_down[...],
    )
    both = f32dot(place[...], result)
    keep[...] = both[:PLANE].astype(jnp.bfloat16)
    send[...] = both[PLANE:].astype(jnp.bfloat16)


def merge_kernel(mine, theirs, spread, out):
    both = f32dot(spread[:, :PLANE], mine[...]) + f32dot(spread[:, PLANE:], theirs[...])
    out[...] = both.astype(jnp.bfloat16)


def call(kernel, outs, args, scratch=(), flops=0, skip=(), wide=(), vmem=24 << 20):
    specs = [
        pl.BlockSpec(memory_space=pltpu.HBM if k in skip else pltpu.VMEM) for k in range(len(args))
    ]
    return pl.pallas_call(
        kernel,
        out_shape=[
            jax.ShapeDtypeStruct(s, jnp.float32 if k in wide else jnp.bfloat16)
            for k, s in enumerate(outs)
        ],
        in_specs=specs,
        out_specs=[pl.BlockSpec(memory_space=pltpu.VMEM)] * len(outs),
        scratch_shapes=list(scratch),
        compiler_params=pltpu.CompilerParams(vmem_limit_bytes=vmem),
        cost_estimate=pl.CostEstimate(flops=flops, bytes_accessed=1 << 20, transcendentals=0),
    )(*args)


def routes(mesh_shape):
    n_lat, n_lon, n_lev = mesh_shape

    ends = (0, n_lat - 1)

    def pairs(move, rows=range(n_lat)):
        flat = lambda i, j, l: ((i % n_lat) * n_lon + j % n_lon) * n_lev + l
        return [
            (flat(i, j, l), flat(*move(i, j, l)))
            for i in rows
            for j in range(n_lon)
            for l in range(n_lev)
        ]

    lat_b = lambda i: i + 1 if i % 2 else i - 1
    lon_b = lambda j, l: j + 1 if (l + j) % 2 else j - 1
    return {
        "lev": pairs(lambda i, j, l: (i, j, l ^ 1)),
        "lon": pairs(lambda i, j, l: (i, lon_b(j, l), l)),
        "lat_a": pairs(lambda i, j, l: (i ^ 1, j, l)),
        "lat_b": pairs(lambda i, j, l: (lat_b(i), j, l)),
        "corner": pairs(lambda i, j, l: (lat_b(i), j, l), range(1, n_lat - 1)),
        "end": pairs(lambda i, j, l: (lat_b(i), lon_b(j, l), l), ends),
    }


def shards(mesh_shape, tokens, norm_gain, norm_offset, w_qkv, w_proj, w_up, w_down, rel_bias):
    send_to = routes(mesh_shape)
    swap = lambda x, name: lax.ppermute(x, AXES, send_to[name])
    norms = (norm_gain, norm_offset)
    raw = tuple(
        pltpu.with_memory_space_constraint(w, pltpu.HBM) for w in (w_qkv, w_proj, w_up, w_down)
    )
    shapes = [w.shape[1:] for w in raw]
    sems = [pltpu.SemaphoreType.DMA((len(raw) + 1,))]

    plane = tokens.reshape(2 * PLANE, D)
    (cut,) = call(cut_kernel, [(PLANE, D)], (plane,), flops=10**7)
    other = swap(cut, "lev")
    entries = rel_bias.reshape(2 * HEADS, rel_bias.shape[-1])
    pick, feat_first, bias_first, table, *weights = call(
        prepare_first,
        [(WROWS, 3 * PLANE), (KEYS, 128), (WROWS, HEADS * 128), (FROWS * 2 * HEADS, 128)] + shapes,
        (pltpu.with_memory_space_constraint(entries, pltpu.HBM),) + raw,
        scratch=[pltpu.VMEM(entries.shape, jnp.float32)] + sems,
        flops=10**8,
        skip=(0, 1, 2, 3, 4),
        wide=(3,),
    )
    first, near, far, last = call(
        first_kernel,
        [(WROWS, D), (HALF, D), (HALF, D), (QPAD, D)],
        (plane, other, pick, bias_first, feat_first) + norms + tuple(weights),
        flops=2 * 10**9,
    )

    lon_a = swap(near, "lev")
    corner_end = swap(last, "end")
    lon_b = swap(far, "lon")
    prepared = []
    for early in (True, False):
        made = call(
            functools.partial(prepare_if, early),
            [(4, KEYS, 128), (WROWS, HEADS * 128), (2 * PLANE, WROWS), (2 * PLANE, 2 * PLANE)]
            + [(WROWS, D), (WROWS, 2 * D)]
            + shapes,
            (first, table) + norms + raw,
            scratch=sems,
            flops=10**9,
            skip=(4, 5, 6, 7),
        )
        names = ("feat", "bias", "place", "spread", "query", "kv", "qkv", "proj", "up", "down")
        prepared.append(dict(zip(names, made, strict=True)))

    def call_prepared(kernel, outs, common, names, **options):
        picked = tuple(made[name] for made in prepared for name in names)
        body = functools.partial(with_prepared, kernel, len(common), len(names))
        return call(body, outs, common + picked, **options)

    strip_a, strip_b = call(strip_kernel, [(3 * QPAD, D)] * 2, (first, lon_a), flops=10**6)
    lat_b = swap(strip_b, "lat_b")
    lat_a = swap(strip_a, "lat_a")
    mixed, kv_lat = call_prepared(
        near_kernel,
        [(HALF, D), (HALF, 2 * D)],
        (lon_a, lat_a, lat_b) + norms,
        ("query", "kv", "bias", "feat", "qkv"),
        scratch=[pltpu.VMEM((HALF + 6 * QPAD, 2 * D), jnp.bfloat16)],
        flops=2 * 10**9,
    )

    corner_a, corner_b = call(corner_kernel, [(QPAD, D)] * 2, (lon_b,), flops=10**6)
    corner_b = swap(corner_b, "corner")
    corner_a = swap(corner_a, "lat_a")
    keep, send = call_prepared(
        far_kernel,
        [(PLANE, D), (PLANE, D)],
        (first, mixed, kv_lat, lon_b, corner_a, corner_b, corner_end) + norms,
        ("query", "kv", "bias", "feat", "place", "qkv", "proj", "up", "down"),
        flops=2 * 10**9,
    )
    theirs = swap(send, "lev")
    (result,) = call_prepared(
        merge_kernel, [(2 * PLANE, D)], (keep, theirs), ("spread",), flops=10**8
    )
    return result.reshape(1, WLAT, 2 * WLON, D)


def solution(mesh):
    shape = tuple(mesh.shape[name] for name in AXES)
    return jax.shard_map(
        functools.partial(shards, shape),
        mesh=mesh,
        in_specs=(P("lev", "lat", "lon", None), P(), P(), P(), P(), P(), P(), P()),
        out_specs=P("lev", "lat", "lon", None),
        check_vma=False,
    )
```

```python
import functools
import math

import jax
import jax.numpy as jnp
from jax import lax
from jax.experimental import pallas as pl
from jax.experimental.pallas import tpu as pltpu
from jax.sharding import PartitionSpec as P


D = 512
HEADS = 16
HEAD_DIM = 32
WLAT = 6
WLON = 12
WLEV = 2
EPS = 1e-05

QROWS, QCOLS = WLAT // 2, WLON // 2
QPAD = 48
HALF = 2 * QPAD
WROWS = 4 * QPAD
KEYS = 256
PLANE = WLAT * WLON
GROUP = 128 // HEAD_DIM
GROUPS = HEADS // GROUP
FEAT = WLAT + WLON + WLEV
FROWS = 24
NEG = -1e30
ROOT = math.sqrt(HEAD_DIM)
AXES = ("lat", "lon", "lev")


def f32dot(a, b):
    return jnp.dot(a, b, preferred_element_type=jnp.float32)


def layer_norm(values, gain, offset):
    average = jnp.mean(values, axis=-1, keepdims=True)
    centered = values - average
    variance = jnp.mean(centered * centered, axis=-1, keepdims=True)
    return centered * lax.rsqrt(variance + EPS) * gain + offset


def attend(query, bias_q, keys, values, key_feat):
    n = query.shape[0]
    lane_head = lax.broadcasted_iota(jnp.int32, (n, 128), 1) // HEAD_DIM
    pad = jnp.zeros((KEYS - WROWS, 128), jnp.bfloat16)
    ones = jnp.ones((KEYS, 128), jnp.bfloat16)
    outs = []
    for g in range(GROUPS):
        lanes = slice(g * 128, (g + 1) * 128)
        qg = query[:, lanes]
        lhs = jnp.concatenate(
            [
                jnp.concatenate(
                    [
                        jnp.where(lane_head == h, qg, jnp.zeros_like(qg)),
                        bias_q[:, (g * GROUP + h) * 128 : (g * GROUP + h + 1) * 128],
                    ],
                    axis=1,
                )
                for h in range(GROUP)
            ],
            axis=0,
        )
        rhs = jnp.concatenate(
            [jnp.concatenate([keys[:, lanes], pad], axis=0), key_feat], axis=1
        )
        scores = lax.dot_general(
            lhs, rhs, (((1,), (1,)), ((), ())), preferred_element_type=jnp.float32
        )
        top = jnp.max(scores, axis=-1, keepdims=True)
        weight = jnp.exp2((scores - top) * (math.log2(math.e) / ROOT)).astype(jnp.bfloat16)
        vals = jnp.concatenate(
            [jnp.concatenate([values[:, lanes], pad], axis=0), ones], axis=1
        )
        both = f32dot(weight, vals)
        total = both[:n]
        for h in range(1, GROUP):
            here = jnp.concatenate([lane_head, lane_head], axis=1) == h
            total = jnp.where(here, both[h * n : (h + 1) * n], total)
        outs.append((total[:, :128] / total[:, 128:]).astype(jnp.bfloat16))
    return jnp.concatenate(outs, axis=1)


def finish(tokens, mixture, gain, offset, w_proj, w_up, w_down):
    residual = (tokens + f32dot(mixture, w_proj)).astype(jnp.bfloat16).astype(jnp.float32)
    normed = layer_norm(residual, gain, offset).astype(jnp.bfloat16)
    hidden = jax.nn.gelu(f32dot(normed, w_up)).astype(jnp.bfloat16)
    return (residual + f32dot(hidden, w_down)).astype(jnp.bfloat16)


def place_of_device():
    i, j, l = (lax.axis_index(name) for name in AXES)
    wrap = (i == 0) | (i == lax.axis_size("lat") - 1)
    return l % 2, (l + j) % 2, i % 2, wrap


def steps(values, size, count):
    total = jnp.zeros_like(values)
    for k in range(1, count):
        total = total + (values >= k * size).astype(jnp.int32)
    return total


def column(rows):
    return lax.broadcasted_iota(jnp.int32, (rows, 1), 0)


def split_token(t):
    lv = steps(t, QROWS * QCOLS, 3)
    rest = t - lv * (QROWS * QCOLS)
    a = steps(rest, QCOLS, QROWS)
    return lv, a, rest - a * QCOLS


def split_window(w):
    a = steps(w, WLON, WLAT)
    return a, w - a * WLON


def onehot(index, columns):
    lane = lax.broadcasted_iota(jnp.int32, (index.shape[0], columns), 1)
    return (lane == index).astype(jnp.float32).astype(jnp.bfloat16)


def features(a, o, lv, real, width, copies, flags=()):
    lane = lax.broadcasted_iota(jnp.int32, (a.shape[0], width), 1)
    hit = jnp.zeros(lane.shape, jnp.float32)
    for k in range(copies):
        base = k * FEAT
        here = (lane == base + a) | (lane == base + WLAT + o) | (lane == base + WLAT + WLON + lv)
        hit = jnp.where(here, 1.0, hit)
    hit = jnp.where(real, hit, 0.0)
    for k, flag in enumerate(flags):
        hit = jnp.where((lane == copies * FEAT + k) & flag, 1.0, hit)
    return hit.astype(jnp.bfloat16)


def window_rows(side, odd, shifted):
    row = column(WROWS)
    quad = steps(row, QPAD, 4)
    sb = (quad >= 2).astype(jnp.int32)
    sa = quad - 2 * sb
    lv, a, o = split_token(row - quad * QPAD)
    low = jnp.where(sa == 0, 1 - odd, odd)
    east = jnp.where(sb == 0, 1 - side, side)
    if shifted:
        return lv, QROWS * (1 - low) + a, QCOLS * (1 - east) + o
    return lv, QROWS * low + a, QCOLS * east + o


def query_bias(b, spots, table, wrap, bias):
    lane = lax.broadcasted_iota(jnp.int32, (1, 256), 1) % 128
    masks = jnp.where(lane == 3 * FEAT, NEG, 0.0)
    if wrap is not None:
        masks = jnp.where((lane == 3 * FEAT + 1) & wrap, NEG, masks)
    for h in range(0, HEADS, 2):
        pair = [table[pl.ds(b * HEADS + h + k, FROWS, stride=2 * HEADS), :] for k in range(2)]
        rows = jnp.concatenate(pair, axis=1).astype(jnp.bfloat16)
        bias[:, h * 128 : (h + 2) * 128] = (f32dot(spots, rows) + masks).astype(jnp.bfloat16)


def cut_kernel(plane, out):
    _, side, _, _ = place_of_device()
    a, o = split_window(column(PLANE))
    source = a * (2 * WLON) + WLON * (1 - side) + o
    out[...] = f32dot(onehot(source, 2 * PLANE), plane[...]).astype(jnp.bfloat16)


def start_weights(b, sources, targets, sems):
    copies = [
        pltpu.make_async_copy(src.at[b], dst, sems.at[k])
        for k, (src, dst) in enumerate(zip(sources, targets, strict=True))
    ]
    for copy in copies:
        copy.start()
    return copies


def fill_table(scaled, table):
    hi = scaled.astype(jnp.bfloat16)
    rest = scaled - hi.astype(jnp.float32)
    mid = rest.astype(jnp.bfloat16)
    low = (rest - mid.astype(jnp.float32)).astype(jnp.bfloat16)
    rows, count = scaled.shape
    width = FROWS * 128
    n = lax.broadcasted_iota(jnp.int32, (1, width), 1)
    r, c = n // 128, n % 128
    lat = (r < WLAT) & (c < WLAT)
    lon = (r >= WLAT) & (c >= WLAT) & (r < WLAT + WLON) & (c < WLAT + WLON)
    lev = (r >= WLAT + WLON) & (r < FEAT) & (c >= WLAT + WLON) & (c < FEAT)
    start = jnp.where(
        lat,
        WLAT - 1,
        jnp.where(lon, 2 * WLAT + WLON - 2, 2 * WLAT + 2 * WLON + WLEV - 3),
    )
    index = jnp.where(lat | lon | lev, start + r - c, -1)
    entry = lax.broadcasted_iota(jnp.int32, (count, width), 0)
    hit = jnp.where(entry == index, 1.0, 0.0).astype(jnp.bfloat16)
    found = f32dot(jnp.concatenate([hi, mid, low], axis=0), hit)
    total = found[:rows]
    for k in (1, 2):
        total = total + pltpu.roll(found[k * rows : (k + 1) * rows], k * FEAT, 1)
    for r in range(FROWS):
        table[r * rows : (r + 1) * rows] = total[:, r * 128 : (r + 1) * 128]


def prepare_first(
    rel_bias, w_qkv, w_proj, w_up, w_down,
    pick, key_feat, bias, table, v_qkv, v_proj, v_up, v_down, entries, sems,
):
    fetch = pltpu.make_async_copy(rel_bias, entries, sems.at[4])
    fetch.start()
    copies = start_weights(
        0, (w_qkv, w_proj, w_up, w_down), (v_qkv, v_proj, v_up, v_down), sems
    )
    level, side, odd, _ = place_of_device()
    lv, a, o = window_rows(side, odd, False)
    mine = a * (2 * WLON) + WLON * side + o
    source = jnp.where(lv == level, mine, 2 * PLANE + a * WLON + o)
    source = jnp.where(lv < WLEV, source, -1)
    pick[...] = onehot(source, 3 * PLANE)
    real = lv < WLEV
    spots = features(a, o, lv, real, FROWS, 1)
    key_feat[:WROWS] = features(a, o, lv, real, 128, 3, [~real])
    lane = lax.broadcasted_iota(jnp.int32, (KEYS - WROWS, 128), 1)
    key_feat[WROWS:] = jnp.where(lane == 3 * FEAT, 1.0, 0.0).astype(jnp.bfloat16)
    fetch.wait()
    fill_table(entries[...] * ROOT, table)
    query_bias(0, spots, table, None, bias)
    for copy in copies:
        copy.wait()


def on_half(early):
    i, j, l = (lax.axis_index(name) for name in AXES)
    here = (j < lax.axis_size("lon") // 2) & (i < 2) & (i + j + l > 0)
    return here if early else jnp.logical_not(here)


def prepare_if(early, *refs):
    @pl.when(on_half(early))
    def _():
        prepare_second(*refs)


def with_prepared(kernel, common, count, *refs):
    sets = refs[common : common + count], refs[common + count : common + 2 * count]
    for early, prepared in zip((True, False), sets, strict=True):

        @pl.when(on_half(early))
        def _(prepared=prepared):
            kernel(*refs[:common], *prepared, *refs[common + 2 * count :])


def prepare_second(
    own, table, gain, offset, w_qkv, w_proj, w_up, w_down,
    key_feat, bias, place, spread, query, kv, v_qkv, v_proj, v_up, v_down, sems,
):
    copies = start_weights(
        1, (w_qkv, w_proj, w_up, w_down), (v_qkv, v_proj, v_up, v_down), sems
    )
    level, side, odd, wrap = place_of_device()
    lv, a, o = window_rows(side, odd, True)
    spots = features(a, o, lv, lv < WLEV, FROWS, 1)
    query_bias(1, spots, table, wrap, bias)
    row = column(KEYS)
    part = steps(row, QPAD, 5)
    lv, a, o = split_token(row - part * QPAD)
    real = (lv < WLEV) & (part < 4)
    across_lat = (part >= 2).astype(jnp.int32)
    across_lon = ((part == 1) | (part == 3)).astype(jnp.int32)
    for s_lon in range(2):
        for s_lat in range(2):
            own_low = odd if s_lat == 0 else 1 - odd
            own_east = side if s_lon == 0 else 1 - side
            low = jnp.where(across_lat == 1, 1 - own_low, own_low)
            east = jnp.where(across_lon == 1, 1 - own_east, own_east)
            flags = [~real] + ([real & (across_lat == 1)] if s_lat else [])
            key_feat[2 * s_lon + s_lat] = features(
                QROWS * low + a, QCOLS * east + o, lv, real, 128, 3, flags
            )
    row = column(2 * PLANE)
    other = (row >= PLANE).astype(jnp.int32)
    a, o = split_window(row - other * PLANE)
    at_level = jnp.where(other == 1, 1 - level, level)
    low, east = (a >= QROWS).astype(jnp.int32), (o >= QCOLS).astype(jnp.int32)
    sa = jnp.where(low == 1 - odd, 0, 1)
    sb = jnp.where(east == 1 - side, 0, 1)
    target = (2 * sb + sa) * QPAD + at_level * (QROWS * QCOLS)
    place[...] = onehot(target + (a - QROWS * low) * QCOLS + o - QCOLS * east, WROWS)
    a = steps(row, 2 * WLON, WLAT)
    c = row - a * (2 * WLON)
    right = (c >= WLON).astype(jnp.int32)
    at = a * WLON + c - WLON * right
    spread[...] = onehot(jnp.where(right == side, at, PLANE + at), 2 * PLANE)
    normed = layer_norm(own[...].astype(jnp.float32), gain[1, 0:1], offset[1, 0:1])
    for copy in copies:
        copy.wait()
    packed = f32dot(normed.astype(jnp.bfloat16), v_qkv[...]).astype(jnp.bfloat16)
    query[...] = packed[:, :D]
    kv[...] = packed[:, D:]


def first_kernel(
    own, other, pick, bias, key_feat, gain, offset, w_qkv, w_proj, w_up, w_down, out, near, far
):
    gain, offset = gain.at[0], offset.at[0]
    tokens = f32dot(pick[:, : 2 * PLANE], own[...]) + f32dot(pick[:, 2 * PLANE :], other[...])
    normed = layer_norm(tokens, gain[0:1], offset[0:1]).astype(jnp.bfloat16)
    packed = f32dot(normed, w_qkv[...]).astype(jnp.bfloat16)
    mixture = attend(
        packed[:, :D], bias, packed[:, D : 2 * D], packed[:, 2 * D :], key_feat[...]
    )
    result = finish(
        tokens, mixture, gain[1:2], offset[1:2], w_proj[...], w_up[...], w_down[...]
    )
    out[...] = result
    near[...] = result[:HALF]
    far[...] = result[HALF:]


def strip_kernel(own, lon, lat_a, lat_b):
    for k, out in enumerate((lat_a, lat_b)):
        for at, (ref, quad) in enumerate(((own, k), (own, 2 + k), (lon, k))):
            out[at * QPAD : (at + 1) * QPAD] = ref[quad * QPAD : (quad + 1) * QPAD]


def corner_kernel(own, lon, lat_a, lat_b):
    _, _, _, wrap = place_of_device()
    lat_a[...] = lon[:QPAD]

    @pl.when(wrap)
    def _():
        lat_b[...] = own[3 * QPAD :]

    @pl.when(jnp.logical_not(wrap))
    def _():
        lat_b[...] = lon[QPAD:]


def near_kernel(
    lon, lat_a, lat_b, gain, offset, query, kv_own, bias, key_feat, w_qkv, mixed, kv_far, kv,
):
    gain, offset = gain.at[1], offset.at[1]
    base = 0
    for ref in (lon, lat_a, lat_b):
        more = layer_norm(ref[...].astype(jnp.float32), gain[0:1], offset[0:1])
        kv[base : base + ref.shape[0]] = f32dot(more.astype(jnp.bfloat16), w_qkv[:, D:]).astype(
            jnp.bfloat16
        )
        base += ref.shape[0]
    parts = []
    for sa in range(2):
        q = slice(sa * QPAD, (sa + 1) * QPAD)
        lat = HALF + sa * 3 * QPAD
        window = jnp.concatenate(
            [kv_own[q], kv[q], kv[lat : lat + QPAD], kv[lat + 2 * QPAD : lat + 3 * QPAD]], axis=0
        )
        parts.append(attend(query[q], bias.at[q], window[:, :D], window[:, D:], key_feat[sa]))
        kv_far[sa * QPAD : (sa + 1) * QPAD] = kv[lat + QPAD : lat + 2 * QPAD]
    mixed[...] = jnp.concatenate(parts, axis=0)


def far_kernel(
    own, mixed, kv_lat, lon, lat_a, lat_b, gain, offset,
    query, kv_own, bias, key_feat, place, w_qkv, w_proj, w_up, w_down, keep, send,
):
    gain, offset = gain.at[1], offset.at[1]
    late = jnp.concatenate([lon[...], lat_a[...], lat_b[...]], axis=0).astype(jnp.float32)
    normed = layer_norm(late, gain[0:1], offset[0:1]).astype(jnp.bfloat16)
    kv = f32dot(normed, w_qkv[:, D:]).astype(jnp.bfloat16)
    parts = []
    for sa in range(2):
        q = slice(sa * QPAD, (sa + 1) * QPAD)
        b = slice(HALF + sa * QPAD, HALF + (sa + 1) * QPAD)
        window = jnp.concatenate(
            [kv_own[b], kv[q], kv_lat[q], kv[(2 + sa) * QPAD : (3 + sa) * QPAD]], axis=0
        )
        parts.append(attend(query[b], bias.at[b], window[:, :D], window[:, D:], key_feat[2 + sa]))
    result = finish(
        own[...].astype(jnp.float32), jnp.concatenate([mixed[...]] + parts, axis=0), gain[1:2],
        offset[1:2], w_proj[...], w_up[...], w_down[...],
    )
    both = f32dot(place[...], result)
    keep[...] = both[:PLANE].astype(jnp.bfloat16)
    send[...] = both[PLANE:].astype(jnp.bfloat16)


def merge_kernel(mine, theirs, spread, out):
    both = f32dot(spread[:, :PLANE], mine[...]) + f32dot(spread[:, PLANE:], theirs[...])
    out[...] = both.astype(jnp.bfloat16)


def call(kernel, outs, args, scratch=(), flops=0, skip=(), wide=(), vmem=24 << 20):
    specs = [
        pl.BlockSpec(memory_space=pltpu.HBM if k in skip else pltpu.VMEM) for k in range(len(args))
    ]
    return pl.pallas_call(
        kernel,
        out_shape=[
            jax.ShapeDtypeStruct(s, jnp.float32 if k in wide else jnp.bfloat16)
            for k, s in enumerate(outs)
        ],
        in_specs=specs,
        out_specs=[pl.BlockSpec(memory_space=pltpu.VMEM)] * len(outs),
        scratch_shapes=list(scratch),
        compiler_params=pltpu.CompilerParams(vmem_limit_bytes=vmem),
        cost_estimate=pl.CostEstimate(flops=flops, bytes_accessed=1 << 20, transcendentals=0),
    )(*args)


def routes(mesh_shape):
    n_lat, n_lon, n_lev = mesh_shape

    def pairs(move):
        flat = lambda i, j, l: ((i % n_lat) * n_lon + j % n_lon) * n_lev + l
        return [
            (flat(i, j, l), flat(*move(i, j, l)))
            for i in range(n_lat)
            for j in range(n_lon)
            for l in range(n_lev)
        ]

    lat_b = lambda i: i + 1 if i % 2 else i - 1
    lon_b = lambda j, l: j + 1 if (l + j) % 2 else j - 1
    ends = (0, n_lat - 1)
    return {
        "lev": pairs(lambda i, j, l: (i, j, l ^ 1)),
        "lon": pairs(lambda i, j, l: (i, lon_b(j, l), l)),
        "lat_a": pairs(lambda i, j, l: (i ^ 1, j, l)),
        "lat_b": pairs(lambda i, j, l: (lat_b(i), j, l)),
        "corner": pairs(lambda i, j, l: (lat_b(i), lon_b(j, l) if i in ends else j, l)),
    }


def shards(mesh_shape, tokens, norm_gain, norm_offset, w_qkv, w_proj, w_up, w_down, rel_bias):
    send_to = routes(mesh_shape)
    swap = lambda x, name: lax.ppermute(x, AXES, send_to[name])
    norms = (norm_gain, norm_offset)
    raw = tuple(
        pltpu.with_memory_space_constraint(w, pltpu.HBM) for w in (w_qkv, w_proj, w_up, w_down)
    )
    shapes = [w.shape[1:] for w in raw]
    sems = [pltpu.SemaphoreType.DMA((len(raw) + 1,))]

    plane = tokens.reshape(2 * PLANE, D)
    (cut,) = call(cut_kernel, [(PLANE, D)], (plane,), flops=10**7)
    other = swap(cut, "lev")
    entries = rel_bias.reshape(2 * HEADS, rel_bias.shape[-1])
    pick, feat_first, bias_first, table, *weights = call(
        prepare_first,
        [(WROWS, 3 * PLANE), (KEYS, 128), (WROWS, HEADS * 128), (FROWS * 2 * HEADS, 128)] + shapes,
        (pltpu.with_memory_space_constraint(entries, pltpu.HBM),) + raw,
        scratch=[pltpu.VMEM(entries.shape, jnp.float32)] + sems,
        flops=10**8,
        skip=(0, 1, 2, 3, 4),
        wide=(3,),
    )
    first, near, far = call(
        first_kernel,
        [(WROWS, D), (HALF, D), (HALF, D)],
        (plane, other, pick, bias_first, feat_first) + norms + tuple(weights),
        flops=2 * 10**9,
    )

    lon_a = swap(near, "lev")
    lon_b = swap(far, "lon")
    prepared = []
    for early in (True, False):
        made = call(
            functools.partial(prepare_if, early),
            [(4, KEYS, 128), (WROWS, HEADS * 128), (2 * PLANE, WROWS), (2 * PLANE, 2 * PLANE)]
            + [(WROWS, D), (WROWS, 2 * D)]
            + shapes,
            (first, table) + norms + raw,
            scratch=sems,
            flops=10**9,
            skip=(4, 5, 6, 7),
        )
        names = ("feat", "bias", "place", "spread", "query", "kv", "qkv", "proj", "up", "down")
        prepared.append(dict(zip(names, made, strict=True)))

    def call_prepared(kernel, outs, common, names, **options):
        picked = tuple(made[name] for made in prepared for name in names)
        body = functools.partial(with_prepared, kernel, len(common), len(names))
        return call(body, outs, common + picked, **options)

    strip_a, strip_b = call(strip_kernel, [(3 * QPAD, D)] * 2, (first, lon_a), flops=10**6)
    lat_b = swap(strip_b, "lat_b")
    lat_a = swap(strip_a, "lat_a")
    mixed, kv_lat = call_prepared(
        near_kernel,
        [(HALF, D), (HALF, 2 * D)],
        (lon_a, lat_a, lat_b) + norms,
        ("query", "kv", "bias", "feat", "qkv"),
        scratch=[pltpu.VMEM((HALF + 6 * QPAD, 2 * D), jnp.bfloat16)],
        flops=2 * 10**9,
    )

    corner_a, corner_b = call(corner_kernel, [(QPAD, D)] * 2, (first, lon_b), flops=10**6)
    corner_b = swap(corner_b, "corner")
    corner_a = swap(corner_a, "lat_a")
    keep, send = call_prepared(
        far_kernel,
        [(PLANE, D), (PLANE, D)],
        (first, mixed, kv_lat, lon_b, corner_a, corner_b) + norms,
        ("query", "kv", "bias", "feat", "place", "qkv", "proj", "up", "down"),
        flops=2 * 10**9,
    )
    theirs = swap(send, "lev")
    (result,) = call_prepared(
        merge_kernel, [(2 * PLANE, D)], (keep, theirs), ("spread",), flops=10**8
    )
    return result.reshape(1, WLAT, 2 * WLON, D)


def solution(mesh):
    shape = tuple(mesh.shape[name] for name in AXES)
    return jax.shard_map(
        functools.partial(shards, shape),
        mesh=mesh,
        in_specs=(P("lev", "lat", "lon", None), P(), P(), P(), P(), P(), P(), P()),
        out_specs=P("lev", "lat", "lon", None),
        check_vma=False,
    )
```
